32 devices in a mesh: tm: 4 (over y, core), space: 8 (over z, x).
Axes of the slice: x: 2, y: 2, z: 4, core: 2. Of those that a mesh axis runs over, the one named last changes fastest.
Arguments:
- first_state: float32 [16, 64, 256], P(None, 'space'), may hold values from -6 to 6
- time_embed: float32 [4, 320], P('tm'), may hold values from -6 to 6
- drift_scale: float32 [4], P('tm'), may hold values from 0.05 to 0.25
- state_decay: float32 [4], P('tm'), may hold values from 0.01 to 0.1
- lift_weight: bfloat16 [320, 16], replicated, may hold values from -1.5 to 1.5
- conv_one: bfloat16 [3, 3, 320, 320], replicated, may hold values from -0.109375 to 0.109375
- conv_two: bfloat16 [3, 3, 320, 320], replicated, may hold values from -0.109375 to 0.109375
- project_weight: bfloat16 [16, 320], replicated, may hold values from -0.3125 to 0.3125
Outputs:
- trajectory: float32 [4, 16, 64, 256], P('tm', None, 'space')
The draws below stay inside these ranges and needn't reach their ends.
All inputs are finite; a program needn't handle non-finite values.
Results may differ from the reference program's by a relative error of at most 0.0019.
Values may be sent and summed in bfloat16 or wider, within the bound.
A program may use at most 128 MiB of HBM per device.

```python
import math
import jax
import jax.numpy as jnp
from jax import lax

C = 16
F = 320
W = 256
ITERS = 2
H = 64
STEPS = 4


def shard_levels(own_key, dims, shards, least, high):
    gain = 1.0
    for position, parts in shards:
        heights = jax.random.uniform(jax.random.fold_in(jax.random.fold_in(own_key, 6), position), (parts,), jnp.float32, least / len(shards), high / len(shards))
        gain = gain * jnp.repeat(jnp.exp(heights), dims[position] // parts).reshape((-1,) + (1,) * (len(dims) - 1 - position))
    return gain


def scatter_about(own_key, extent, scale, most, pieces=(), kind=jnp.bfloat16):
    array = jax.random.normal(own_key, extent, jnp.float32) * scale
    if len(pieces) > 0:
        array = shard_levels(own_key, extent, pieces, -0.22, 0.18) * array
    return jnp.clip(array, min=-most, max=most).astype(kind)


def setup_inputs(seed: int = 0) -> dict:
    key_of = jax.random.split(jax.random.key(seed), 9)
    return {
        "first_state": scatter_about(key_of[0], (C, H, W), 1.0, 6.0, ((1, 8),), jnp.float32),
        "time_embed": scatter_about(key_of[1], (STEPS, F), 1.0, 6.0, ((0, 4),), jnp.float32),
        "drift_scale": jnp.clip(jnp.exp(math.log(0.25) - 1.609438 * jax.random.uniform(key_of[2], (STEPS,), jnp.float32) ** shard_levels(key_of[2], (STEPS,), ((0, 4),), -0.2, 0.2)), 0.05, 0.25),
        "state_decay": jnp.clip(jnp.exp(math.log(0.1) - 2.3025851 * jax.random.uniform(key_of[3], (STEPS,), jnp.float32) ** shard_levels(key_of[3], (STEPS,), ((0, 4),), -0.2, 0.2)), 0.01, 0.1),
        "lift_weight": scatter_about(key_of[4], (F, C), C ** -0.5, 1.5),
        "conv_one": scatter_about(key_of[5], (3, 3, F, F), (9 * F) ** -0.5, 0.109375),
        "conv_two": scatter_about(key_of[6], (3, 3, F, F), (9 * F) ** -0.5, 0.109375),
        "project_weight": scatter_about(key_of[7], (C, F), F ** -0.5, 0.3125),
    }


def shift_columns(field, col_tap):
    spread = [(0, 0)] * (field.ndim - 1)
    if col_tap == 0:
        return jnp.pad(field[..., :-1], spread + [(1, 0)])
    if col_tap == 2:
        return jnp.pad(field[..., 1:], spread + [(0, 1)])
    return field


def convolve(active, weight):
    chans, height, width = active.shape
    padded = jnp.pad(active, ((0, 0), (1, 1), (0, 0)))
    total = jnp.zeros((weight.shape[2], height * width), jnp.float32)
    for row_tap in range(3):
        rows_view = padded[:, row_tap:row_tap + height]
        for col_tap in range(3):
            tile = shift_columns(rows_view, col_tap).reshape(chans, -1)
            total = total + jnp.dot(weight[row_tap, col_tap], tile, preferred_element_type=jnp.float32)
    return total.reshape(-1, height, width)


def denoise_one(state, embed, lift_weight, conv_one, conv_two, project_weight):
    chans, height, width = state.shape
    flat = state.astype(jnp.bfloat16).reshape(chans, -1)
    lifted = jnp.dot(lift_weight, flat, preferred_element_type=jnp.float32).reshape(-1, height, width)
    lifted = lifted + embed[:, None, None]
    first = lifted + convolve(jax.nn.silu(lifted).astype(jnp.bfloat16), conv_one)
    second = first + convolve(jax.nn.silu(first).astype(jnp.bfloat16), conv_two)
    active = jax.nn.silu(second).astype(jnp.bfloat16).reshape(second.shape[0], -1)
    return jnp.dot(project_weight, active, preferred_element_type=jnp.float32).reshape(chans, height, width)


def reference(first_state, time_embed, drift_scale, state_decay, lift_weight, conv_one, conv_two, project_weight):
    states = jnp.broadcast_to(first_state[None], (STEPS,) + first_state.shape)
    running = jnp.zeros_like(states)
    for sweep in range(ITERS):
        def single(pair):
            return denoise_one(pair[0], pair[1], lift_weight, conv_one, conv_two, project_weight)

        outputs = lax.map(single, (states, time_embed))
        drifts = drift_scale[:, None, None, None] * outputs - state_decay[:, None, None, None] * states
        running = jnp.cumsum(drifts, axis=0)
        if sweep + 1 < ITERS:
            shifted = jnp.concatenate([jnp.zeros_like(running[:1]), running[:-1]], axis=0)
            states = first_state[None] + shifted
    return first_state[None] + running
```

```python
import functools

import jax
import jax.numpy as jnp
from jax import lax
from jax.experimental import pallas as pl
from jax.experimental.pallas import tpu as pltpu
from jax.sharding import PartitionSpec as P

ITERS = 2
TILE = 256
EXTRA = 64
MESH = pl.DeviceIdType.MESH


def gate(half):
    return half + half * jnp.tanh(half)


def split_three(value):
    high = value.astype(jnp.bfloat16)
    left = value - high.astype(jnp.float32)
    mid = left.astype(jnp.bfloat16)
    low = (left - mid.astype(jnp.float32)).astype(jnp.bfloat16)
    return high, mid, low


def kernel(
    steps,
    tiles,
    x_hbm,
    embed_hbm,
    scale_ref,
    decay_ref,
    lift_hbm,
    project_hbm,
    conv_one_hbm,
    conv_two_hbm,
    out_ref,
    x_ref,
    embed_ref,
    lift_ref,
    project_ref,
    raw_one,
    raw_two,
    u_one,
    u_two,
    lift_rows,
    main_one,
    rest_one,
    main_two,
    rest_two,
    first,
    prods,
    act_three,
    turned,
    rows_f32,
    state_rows,
    xb_rows,
    drift_out,
    drift_in,
    load_sem,
    halo_send,
    halo_recv,
    drift_send,
    drift_recv,
):
    chans, height, width = x_ref.shape
    feats = lift_ref.shape[1]
    side = width // 2
    main = feats // TILE * TILE
    rest = feats - main
    depth = 3 * feats
    chunk = 64
    tm = lax.axis_index("tm")
    space = lax.axis_index("space")
    has_up = space > 0
    has_down = space < tiles - 1

    pairs = (
        (x_hbm, x_ref),
        (embed_hbm, embed_ref),
        (lift_hbm, lift_ref),
        (project_hbm, project_ref),
        (conv_one_hbm, raw_one),
        (conv_two_hbm, raw_two),
    )
    loads = [pltpu.make_async_copy(a, b, load_sem.at[i]) for i, (a, b) in enumerate(pairs)]
    for load in loads:
        load.start()

    barrier = pltpu.get_barrier_semaphore()
    for shift in range(1, steps):
        other = lax.rem(tm + shift, steps)
        pl.semaphore_signal(barrier, inc=1, device_id=(other, space), device_id_type=MESH)

    @pl.when(has_up)
    def _():
        pl.semaphore_signal(barrier, inc=1, device_id=(tm, space - 1), device_id_type=MESH)

    @pl.when(has_down)
    def _():
        pl.semaphore_signal(barrier, inc=1, device_id=(tm, space + 1), device_id_type=MESH)

    def clear_halo(start):
        for sweep in range(ITERS):
            for index in (start, start + 1):
                xb_rows[sweep, index] = jnp.zeros((chans, width), jnp.bfloat16)

    @pl.when(space == 0)
    def _():
        clear_halo(0)

    @pl.when(space == tiles - 1)
    def _():
        clear_halo(height + 2)

    def halo_copies(sweep):
        up = pltpu.make_async_remote_copy(
            src_ref=xb_rows.at[sweep, pl.ds(2, 2)],
            dst_ref=xb_rows.at[sweep, pl.ds(height + 2, 2)],
            send_sem=halo_send.at[sweep, 0],
            recv_sem=halo_recv.at[sweep, 1],
            device_id=(tm, space - 1),
            device_id_type=MESH,
        )
        down = pltpu.make_async_remote_copy(
            src_ref=xb_rows.at[sweep, pl.ds(height, 2)],
            dst_ref=xb_rows.at[sweep, pl.ds(0, 2)],
            send_sem=halo_send.at[sweep, 1],
            recv_sem=halo_recv.at[sweep, 0],
            device_id=(tm, space + 1),
            device_id_type=MESH,
        )
        return up, down

    def send_halo(sweep):
        up, down = halo_copies(sweep)

        @pl.when(has_up)
        def _():
            up.start()

        @pl.when(has_down)
        def _():
            down.start()

    def wait_halo(sweep):
        up, down = halo_copies(sweep)

        @pl.when(has_up)
        def _():
            down.wait_recv()

        @pl.when(has_down)
        def _():
            up.wait_recv()

    def drift_copy(sweep, shift, pair):
        return pltpu.make_async_remote_copy(
            src_ref=drift_out.at[sweep, pl.ds(2 * pair, 2)],
            dst_ref=drift_in.at[sweep, shift - 1, pl.ds(2 * pair, 2)],
            send_sem=drift_send.at[sweep, shift - 1, pair],
            recv_sem=drift_recv.at[sweep, shift - 1, pair],
            device_id=(tm + shift, space),
            device_id_type=MESH,
        )

    def send_drift(sweep, pair):
        for shift in range(1, steps):

            @pl.when(tm + shift < steps)
            def _():
                drift_copy(sweep, shift, pair).start()

    def wait_drift(sweep, pair):
        for shift in range(1, steps):

            @pl.when(tm >= shift)
            def _():
                drift_copy(sweep, shift, pair).wait_recv()

    def earlier(sweep, row):
        total = jnp.zeros((chans, width), jnp.float32)
        for shift in range(1, steps):
            total = total + jnp.where(tm >= shift, drift_in[sweep, shift - 1, row], 0.0)
        return total

    lane = lax.broadcasted_iota(jnp.int32, (chunk, side), 1)
    zero = jnp.zeros((), jnp.bfloat16)
    ones = jnp.ones((EXTRA - chans, side), jnp.bfloat16)

    def spread(mains, rests, index, start, act):
        value = act.astype(jnp.bfloat16)
        even, odd = value[:, :side], value[:, side:]
        before = jnp.where(lane == 0, zero, pltpu.roll(odd, 1, 1))
        after = jnp.where(lane == side - 1, zero, pltpu.roll(even, side - 1, 1))
        parts = (before - odd, even + odd, odd - even, after - even)
        for m, part in enumerate(parts):
            if start < main:
                place = index * main + start
                mains[m, place : place + chunk, :] = part
            else:
                place = index * rest + start - main
                rests[m, place : place + chunk, :] = part

    def extra(sweep, index, odd):
        xb = xb_rows[sweep, index]
        return jnp.concatenate([xb[:, side:] if odd else xb[:, :side], ones], axis=0)

    def product(weight, mains, rests, m, pair, sweep=None):
        taken = []
        used = depth + EXTRA
        for index in pair:
            pieces = [
                mains[m, index * main : (index + 3) * main, :],
                rests[m, index * rest : (index + 3) * rest, :],
            ]
            if sweep is not None and m in (0, 3):
                pieces.append(extra(sweep, index + 1, m == 3))
            else:
                pieces.append(jnp.zeros((EXTRA, side), jnp.bfloat16))
            taken.append(jnp.concatenate(pieces, axis=0))
        return jnp.dot(
            weight[m, :, :used],
            jnp.concatenate(taken, axis=1),
            preferred_element_type=jnp.float32,
        )

    def lift(sweep, pair):
        tall = jnp.ones((128 - chans, 2 * width), jnp.bfloat16)
        xb = jnp.concatenate([xb_rows[sweep, index] for index in pair], axis=1)
        return jnp.dot(
            lift_rows[...],
            jnp.concatenate([xb, tall], axis=0),
            preferred_element_type=jnp.float32,
        )

    def build_items(sweep, pair):
        value = lift(sweep, pair)

        def item(half, index, start):
            act = gate(value[start : start + chunk, half * width : (half + 1) * width])
            if index < 2:
                act = jnp.where(has_up, act, 0.0)
            if index >= height + 2:
                act = jnp.where(has_down, act, 0.0)
            spread(main_one, rest_one, index, start, act)

        return [
            functools.partial(item, half, index, start)
            for half, index in enumerate(pair)
            for start in range(0, feats, chunk)
        ]

    def joined(slot, half, start):
        lanes = slice(half * side, (half + 1) * side)
        m0, m1, m2, m3 = [prods[slot, m, start : start + chunk, lanes] for m in range(4)]
        return jnp.concatenate([m0 + m1 + m2, m1 - m2 + m3], axis=1)

    def activate_items(pair, slot):
        def item(half, index, start):
            value = joined(slot, half, start)
            if 0 < index <= height:
                first[index, start : start + chunk, :] = value
            act = gate(value)
            if index == 0:
                act = jnp.where(has_up, act, 0.0)
            if index == height + 1:
                act = jnp.where(has_down, act, 0.0)
            spread(main_two, rest_two, index, start, act)

        return [
            functools.partial(item, half, index, start)
            for half, index in enumerate(pair)
            for start in range(0, feats, chunk)
        ]

    def finish_items(sweep, pair, slot):
        def item(half, row, start):
            act = gate(first[row + 1, start : start + chunk, :] + joined(slot, half, start))
            act_three[
                slot, start : start + chunk, half * width : (half + 1) * width
            ] = act.astype(jnp.bfloat16)

        def last():
            out = jnp.dot(
                project_ref[...], act_three[slot], preferred_element_type=jnp.float32
            )
            for half, row in enumerate(pair):
                part = out[:, half * width : (half + 1) * width]
                drift_out[sweep, row] = scale_ref[0] * part - decay_ref[0] * state_rows[row]
            send_drift(sweep, pair[0] // 2)

        return [
            functools.partial(item, half, row, start)
            for half, row in enumerate(pair)
            for start in range(0, feats, chunk)
        ] + [last]

    def weight_items(raw, weight):
        def item(p):
            taps = [raw[p, q].astype(jnp.float32) for q in range(3)]
            outer = taps[0] + taps[2]
            filtered = (
                0.5 * taps[0],
                0.25 * (outer + taps[1]),
                0.25 * (outer - taps[1]),
                0.5 * taps[2],
            )
            for m, value in enumerate(filtered):
                value = value.astype(jnp.bfloat16)
                weight[m, :, p * main : (p + 1) * main] = value[:, :main]
                place = 3 * main + p * rest
                weight[m, :, place : place + rest] = value[:, main:]

        return [functools.partial(item, p) for p in range(3)]

    def take_states(sweep, pair):
        wait_drift(sweep - 1, pair)
        for row in (2 * pair, 2 * pair + 1):
            state = rows_f32[row] + earlier(sweep - 1, row)
            state_rows[row] = state
            xb_rows[sweep, row + 2] = state.astype(jnp.bfloat16)

    def run(items):
        for item in items:
            item()

    def turn(slot, products, items):
        count = len(products)
        for m, make in enumerate(products):
            prods[slot, m] = make()
            run(items[m * len(items) // count : (m + 1) * len(items) // count])

    def one_sweep(sweep):
        if sweep > 0:
            for pair in range(2):
                take_states(sweep, pair)
        run(build_items(sweep, (2, 3)))
        run(build_items(sweep, (4, 5)))
        if sweep == 0:
            loads[4].wait()
            run(weight_items(raw_one, u_one))

        order = [(index, index + 1) for index in range(2, height, 2)]
        order += [(1, height), (0, height + 1)]
        builds = [(index + 4, index + 5) for index in range(2, height - 2, 2)]
        builds += [(1, height + 2), (0, height + 3), ()]
        before = None
        for place, pair in enumerate(order):
            fresh = builds[place]
            items = []
            if place == 0 and sweep > 0:
                for rest_pair in range(height // 2 - 1, 1, -1):
                    take_states(sweep, rest_pair)
                send_halo(sweep)
            if 1 in fresh:
                wait_halo(sweep)
            if fresh:
                items += build_items(sweep, fresh)
            if before is not None:
                items += activate_items(before, 1 - place % 2)
            if sweep == 0 and place == 1:
                loads[5].wait()
            if sweep == 0 and place >= 1:
                items += weight_items(raw_two, u_two)[place - 1 : place]
            turn(
                place % 2,
                [
                    functools.partial(product, u_one, main_one, rest_one, m, pair, sweep)
                    for m in range(4)
                ],
                items,
            )
            before, slot = pair, place % 2

        edges = (0, 1, height - 2, height - 1)
        middle = tuple(range(2, height - 2))
        order = [middle[:2], edges[:2], edges[2:]]
        order += [middle[place : place + 2] for place in range(2, len(middle), 2)]
        done = None
        for pair in order:
            if done is None:
                items = activate_items(before, slot)
            else:
                items = finish_items(sweep, done, slot)
            slot = 1 - slot
            turn(
                slot,
                [
                    functools.partial(product, u_two, main_two, rest_two, m, pair)
                    for m in range(4)
                ],
                items,
            )
            done = pair
        run(finish_items(sweep, done, slot))

    def parted(out_of):
        down = lax.broadcasted_iota(jnp.int32, (width, width), 0)
        across = lax.broadcasted_iota(jnp.int32, (width, width), 1)
        place, column = (down, across) if out_of else (across, down)
        source = jnp.where(place < side, 2 * place, 2 * (place - side) + 1)
        return jnp.where(source == column, 1.0, 0.0).astype(jnp.bfloat16)

    def reorder(value, matrix):
        return jnp.dot(
            jnp.concatenate(split_three(value), axis=1),
            jnp.concatenate([matrix] * 3, axis=0),
            preferred_element_type=jnp.float32,
        )

    into = parted(False)
    loads[0].wait()
    ordered = reorder(x_ref[...].reshape(chans * height, width), into)
    turned[...] = ordered.reshape(chans, height, width)
    for row in range(height):
        value = turned[:, row, :]
        rows_f32[row] = value
        state_rows[row] = value
        xb_rows[0, row + 2] = value.astype(jnp.bfloat16)
    greeted = (steps - 1) + jnp.where(has_up, 1, 0) + jnp.where(has_down, 1, 0)
    pl.semaphore_wait(barrier, greeted)
    send_halo(0)
    for load in loads[1:4]:
        load.wait()
    wide = (-feats) % 128
    parts = [
        part.astype(jnp.float32)
        for part in split_three(jnp.pad(embed_ref[...], ((0, 0), (0, wide))))
    ]
    line = lax.broadcasted_iota(jnp.int32, (128 - chans, feats + wide), 0)
    under = jnp.zeros((128 - chans, feats + wide), jnp.float32)
    for place, part in enumerate(parts):
        under = jnp.where(line == place, part, under)
    over = jnp.pad(lift_ref[...].astype(jnp.float32), ((0, 0), (0, wide)))
    stacked = jnp.transpose(jnp.concatenate([over, under], axis=0))[:feats]
    lift_rows[...] = (0.5 * stacked).astype(jnp.bfloat16)
    for m in range(4):
        none = jnp.zeros((feats, EXTRA), jnp.bfloat16)
        u_one[m, :, depth : depth + EXTRA] = lift_rows[:, :EXTRA] if m in (0, 3) else none
        u_two[m, :, depth : depth + EXTRA] = none

    for sweep in range(ITERS):
        one_sweep(sweep)

    for pair in range(height // 2):
        wait_drift(ITERS - 1, pair)
    for row in range(height):
        turned[:, row, :] = drift_out[ITERS - 1, row] + earlier(ITERS - 1, row)
    total = reorder(turned[...].reshape(chans * height, width), parted(True))
    out_ref[0] = x_ref[...] + total.reshape(chans, height, width)

    for sweep in range(ITERS):
        up, down = halo_copies(sweep)

        @pl.when(has_up)
        def _():
            up.wait_send()

        @pl.when(has_down)
        def _():
            down.wait_send()

        for shift in range(1, steps):
            for pair in range(height // 2):

                @pl.when(tm + shift < steps)
                def _():
                    drift_copy(sweep, shift, pair).wait_send()


def solution(mesh):
    steps, tiles = mesh.shape["tm"], mesh.shape["space"]

    def per_device(
        first_state,
        time_embed,
        drift_scale,
        state_decay,
        lift_weight,
        conv_one,
        conv_two,
        project_weight,
    ):
        chans, height, width = first_state.shape
        feats = lift_weight.shape[0]
        main = feats // TILE * TILE
        rest = feats - main
        depth = 3 * feats
        side = width // 2
        lines = pl.cdiv(depth + EXTRA, 128)
        wide = (lines + 1 - lines % 2) * 128
        peers = max(steps - 1, 1)
        vmem = pl.BlockSpec(memory_space=pltpu.VMEM)
        smem = pl.BlockSpec(memory_space=pltpu.SMEM)
        hbm = pl.BlockSpec(memory_space=pltpu.HBM)
        return pl.pallas_call(
            functools.partial(kernel, steps, tiles),
            out_shape=jax.ShapeDtypeStruct((1, chans, height, width), jnp.float32),
            in_specs=[hbm, hbm, smem, smem, hbm, hbm, hbm, hbm],
            out_specs=vmem,
            scratch_shapes=[
                pltpu.VMEM((chans, height, width), jnp.float32),
                pltpu.VMEM((1, feats), jnp.float32),
                pltpu.VMEM((chans, feats), jnp.bfloat16),
                pltpu.VMEM((chans, feats), jnp.bfloat16),
                pltpu.VMEM((3, 3, feats, feats), jnp.bfloat16),
                pltpu.VMEM((3, 3, feats, feats), jnp.bfloat16),
                pltpu.VMEM((4, feats, wide), jnp.bfloat16),
                pltpu.VMEM((4, feats, wide), jnp.bfloat16),
                pltpu.VMEM((feats, 128), jnp.bfloat16),
                pltpu.VMEM((4, (height + 4) * main, side), jnp.bfloat16),
                pltpu.VMEM((4, (height + 4) * rest, side), jnp.bfloat16),
                pltpu.VMEM((4, (height + 2) * main, side), jnp.bfloat16),
                pltpu.VMEM((4, (height + 2) * rest, side), jnp.bfloat16),
                pltpu.VMEM((height + 2, feats, width), jnp.float32),
                pltpu.VMEM((2, 4, feats, width), jnp.float32),
                pltpu.VMEM((2, feats, 2 * width), jnp.bfloat16),
                pltpu.VMEM((chans, height, width), jnp.float32),
                pltpu.VMEM((height, chans, width), jnp.float32),
                pltpu.VMEM((height, chans, width), jnp.float32),
                pltpu.VMEM((ITERS, height + 4, chans, width), jnp.bfloat16),
                pltpu.VMEM((ITERS, height, chans, width), jnp.float32),
                pltpu.VMEM((ITERS, peers, height, chans, width), jnp.float32),
                pltpu.SemaphoreType.DMA((6,)),
                pltpu.SemaphoreType.DMA((ITERS, 2)),
                pltpu.SemaphoreType.DMA((ITERS, 2)),
                pltpu.SemaphoreType.DMA((ITERS, peers, height // 2)),
                pltpu.SemaphoreType.DMA((ITERS, peers, height // 2)),
            ],
            compiler_params=pltpu.CompilerParams(
                collective_id=0, has_side_effects=True, vmem_limit_bytes=67043328
            ),
        )(
            first_state,
            time_embed,
            drift_scale,
            state_decay,
            lift_weight.T,
            project_weight,
            conv_one,
            conv_two,
        )

    in_specs = (P(None, "space", None), P("tm", None), P("tm"), P("tm"), P(), P(), P(), P())
    return jax.shard_map(
        per_device,
        mesh=mesh,
        in_specs=in_specs,
        out_specs=P("tm", None, "space", None),
        check_vma=False,
    )
```

```python
import functools

import jax
import jax.numpy as jnp
from jax import lax
from jax.experimental import pallas as pl
from jax.experimental.pallas import tpu as pltpu
from jax.sharding import PartitionSpec as P

ITERS = 2
TILE = 256
EXTRA = 64
MESH = pl.DeviceIdType.MESH


def gate(half):
    return half + half * jnp.tanh(half)


def split_three(value):
    high = value.astype(jnp.bfloat16)
    left = value - high.astype(jnp.float32)
    mid = left.astype(jnp.bfloat16)
    low = (left - mid.astype(jnp.float32)).astype(jnp.bfloat16)
    return high, mid, low


def kernel(
    steps,
    tiles,
    x_hbm,
    embed_hbm,
    scale_ref,
    decay_ref,
    lift_hbm,
    project_hbm,
    conv_one_hbm,
    conv_two_hbm,
    out_ref,
    x_ref,
    embed_ref,
    lift_ref,
    project_ref,
    raw_one,
    raw_two,
    u_one,
    u_two,
    lift_rows,
    main_one,
    rest_one,
    main_two,
    rest_two,
    first,
    prods,
    act_three,
    turned,
    rows_f32,
    state_rows,
    xb_rows,
    drift_own,
    drift_out,
    drift_in,
    load_sem,
    halo_send,
    halo_recv,
    drift_send,
    drift_recv,
):
    chans, height, width = x_ref.shape
    feats = lift_ref.shape[1]
    side = width // 2
    main = feats // TILE * TILE
    rest = feats - main
    depth = 3 * feats
    chunk = 64
    tm = lax.axis_index("tm")
    space = lax.axis_index("space")
    has_up = space > 0
    has_down = space < tiles - 1

    pairs = [(x_hbm, x_ref), (embed_hbm, embed_ref), (lift_hbm, lift_ref)]
    pairs += [(project_hbm, project_ref)]
    pairs += [(conv_one_hbm.at[p], raw_one.at[p]) for p in range(3)]
    pairs += [(conv_two_hbm.at[p], raw_two.at[p]) for p in range(3)]
    loads = [pltpu.make_async_copy(a, b, load_sem.at[i]) for i, (a, b) in enumerate(pairs)]
    for load in loads[:7]:
        load.start()

    barrier = pltpu.get_barrier_semaphore()
    for shift in range(1, steps):
        other = lax.rem(tm + shift, steps)
        pl.semaphore_signal(barrier, inc=1, device_id=(other, space), device_id_type=MESH)

    @pl.when(has_up)
    def _():
        pl.semaphore_signal(barrier, inc=1, device_id=(tm, space - 1), device_id_type=MESH)

    @pl.when(has_down)
    def _():
        pl.semaphore_signal(barrier, inc=1, device_id=(tm, space + 1), device_id_type=MESH)

    def clear_halo(start):
        for sweep in range(ITERS):
            for index in (start, start + 1):
                xb_rows[sweep, index] = jnp.zeros((chans, width), jnp.bfloat16)

    @pl.when(space == 0)
    def _():
        clear_halo(0)

    @pl.when(space == tiles - 1)
    def _():
        clear_halo(height + 2)

    def halo_copies(sweep):
        up = pltpu.make_async_remote_copy(
            src_ref=xb_rows.at[sweep, pl.ds(2, 2)],
            dst_ref=xb_rows.at[sweep, pl.ds(height + 2, 2)],
            send_sem=halo_send.at[sweep, 0],
            recv_sem=halo_recv.at[sweep, 1],
            device_id=(tm, space - 1),
            device_id_type=MESH,
        )
        down = pltpu.make_async_remote_copy(
            src_ref=xb_rows.at[sweep, pl.ds(height, 2)],
            dst_ref=xb_rows.at[sweep, pl.ds(0, 2)],
            send_sem=halo_send.at[sweep, 1],
            recv_sem=halo_recv.at[sweep, 0],
            device_id=(tm, space + 1),
            device_id_type=MESH,
        )
        return up, down

    def send_up(sweep):
        @pl.when(has_up)
        def _():
            halo_copies(sweep)[0].start()

    def send_down(sweep):
        @pl.when(has_down)
        def _():
            halo_copies(sweep)[1].start()

    def drift_copy(sweep, shift, pair):
        return pltpu.make_async_remote_copy(
            src_ref=drift_out.at[sweep, pl.ds(2 * pair, 2)],
            dst_ref=drift_in.at[sweep, shift - 1, pl.ds(2 * pair, 2)],
            send_sem=drift_send.at[sweep, shift - 1, pair],
            recv_sem=drift_recv.at[sweep, shift - 1, pair],
            device_id=(tm + shift, space),
            device_id_type=MESH,
        )

    def send_drift(sweep, pair):
        for shift in range(1, steps):

            @pl.when(tm + shift < steps)
            def _():
                drift_copy(sweep, shift, pair).start()

    def wait_drift(sweep, pair):
        for shift in range(1, steps):

            @pl.when(tm >= shift)
            def _():
                drift_copy(sweep, shift, pair).wait_recv()

    def earlier(sweep, row):
        total = jnp.zeros((chans, width), jnp.float32)
        for shift in range(1, steps):
            part = drift_in[sweep, shift - 1, row].astype(jnp.float32)
            total = total + jnp.where(tm >= shift, part, 0.0)
        return total

    lane = lax.broadcasted_iota(jnp.int32, (chunk, side), 1)
    zero = jnp.zeros((), jnp.bfloat16)
    ones = jnp.ones((EXTRA - chans, side), jnp.bfloat16)

    def spread(mains, rests, index, start, even, odd):
        even, odd = even.astype(jnp.bfloat16), odd.astype(jnp.bfloat16)
        before = jnp.where(lane == 0, zero, pltpu.roll(odd, 1, 1))
        after = jnp.where(lane == side - 1, zero, pltpu.roll(even, side - 1, 1))
        parts = (before - odd, even + odd, odd - even, after - even)
        for m, part in enumerate(parts):
            if start < main:
                place = index * main + start
                mains[m, place : place + chunk, :] = part
            else:
                place = index * rest + start - main
                rests[m, place : place + chunk, :] = part

    def extra(sweep, index, odd):
        xb = xb_rows[sweep, index]
        return jnp.concatenate([xb[:, side:] if odd else xb[:, :side], ones], axis=0)

    def product(weight, mains, rests, m, pair, sweep=None):
        taken = []
        used = depth + EXTRA
        for index in pair:
            pieces = [
                mains[m, index * main : (index + 3) * main, :],
                rests[m, index * rest : (index + 3) * rest, :],
            ]
            if sweep is not None and m in (0, 3):
                pieces.append(extra(sweep, index + 1, m == 3))
            else:
                pieces.append(jnp.zeros((EXTRA, side), jnp.bfloat16))
            taken.append(jnp.concatenate(pieces, axis=0))
        return jnp.dot(
            weight[m, :, :used],
            jnp.concatenate(taken, axis=1),
            preferred_element_type=jnp.float32,
        )

    def lift(sweep, pair):
        tall = jnp.ones((128 - chans, 2 * width), jnp.bfloat16)
        xb = jnp.concatenate([xb_rows[sweep, index] for index in pair], axis=1)
        return jnp.dot(
            lift_rows[...],
            jnp.concatenate([xb, tall], axis=0),
            preferred_element_type=jnp.float32,
        )

    def build_items(sweep, pair):
        held = []

        def first_item():
            for index in pair:
                reach(sweep, index)
            held.append(lift(sweep, pair))

        def item(half, index, start):
            acts = []
            for lanes in (half * width, half * width + side):
                act = gate(held[0][start : start + chunk, lanes : lanes + side])
                if index < 2:
                    act = jnp.where(has_up, act, 0.0)
                if index >= height + 2:
                    act = jnp.where(has_down, act, 0.0)
                acts.append(act)
            spread(main_one, rest_one, index, start, *acts)

        return [first_item] + [
            functools.partial(item, half, index, start)
            for half, index in enumerate(pair)
            for start in range(0, feats, chunk)
        ]

    def joined(slot, half, start):
        lanes = slice(half * side, (half + 1) * side)
        m0, m1, m2, m3 = [prods[slot, m, start : start + chunk, lanes] for m in range(4)]
        return m0 + m1 + m2, m1 - m2 + m3

    def activate_items(sweep, pair, slot):
        def item(half, index, start):
            values = joined(slot, half, start)
            acts = []
            for place, value in enumerate(values):
                if 0 < index <= height:
                    first[index, start : start + chunk, place * side : (place + 1) * side] = value
                act = gate(value)
                if index == 0:
                    act = jnp.where(has_up, act, 0.0)
                if index == height + 1:
                    act = jnp.where(has_down, act, 0.0)
                acts.append(act)
            spread(main_two, rest_two, index, start, *acts)

        return [
            functools.partial(item, half, index, start)
            for half, index in enumerate(pair)
            for start in range(0, feats, chunk)
        ]

    def finish_items(sweep, pair, slot):
        def item(half, row, start):
            for place, value in enumerate(joined(slot, half, start)):
                lanes = slice(place * side, (place + 1) * side)
                act = gate(first[row + 1, start : start + chunk, lanes] + value)
                lanes = slice(half * width + place * side, half * width + (place + 1) * side)
                act_three[slot, start : start + chunk, lanes] = act.astype(jnp.bfloat16)

        def last():
            out = jnp.dot(
                project_ref[...], act_three[slot], preferred_element_type=jnp.float32
            )
            for half, row in enumerate(pair):
                part = out[:, half * width : (half + 1) * width]
                drift = scale_ref[0] * part - decay_ref[0] * state_rows[row]
                drift_out[sweep, row] = drift.astype(jnp.bfloat16)
                if sweep == ITERS - 1:
                    drift_own[row] = drift
            send_drift(sweep, pair[0] // 2)

        return [
            functools.partial(item, half, row, start)
            for half, row in enumerate(pair)
            for start in range(0, feats, chunk)
        ] + [last]

    def weight_items(raw, weight, number):
        def item(p):
            loads[number + p].wait()
            taps = [raw[p, q].astype(jnp.float32) for q in range(3)]
            outer = taps[0] + taps[2]
            filtered = (
                0.5 * taps[0],
                0.25 * (outer + taps[1]),
                0.25 * (outer - taps[1]),
                0.5 * taps[2],
            )
            for m, value in enumerate(filtered):
                value = value.astype(jnp.bfloat16)
                weight[m, :, p * main : (p + 1) * main] = value[:, :main]
                place = 3 * main + p * rest
                weight[m, :, place : place + rest] = value[:, main:]

        return [functools.partial(item, p) for p in range(3)]

    reached = set()

    def reach(sweep, index):
        if index < 2:
            key = (sweep, "up")
        elif index >= height + 2:
            key = (sweep, "down")
        else:
            key = (sweep, index // 2 - 1)
        if key in reached:
            return
        reached.add(key)
        if index < 2:

            @pl.when(has_up)
            def _():
                halo_copies(sweep)[1].wait_recv()

        elif index >= height + 2:

            @pl.when(has_down)
            def _():
                halo_copies(sweep)[0].wait_recv()

        elif sweep > 0:
            pair = key[1]
            wait_drift(sweep - 1, pair)
            for row in (2 * pair, 2 * pair + 1):
                state = rows_f32[row] + earlier(sweep - 1, row)
                state_rows[row] = state
                xb_rows[sweep, row + 2] = state.astype(jnp.bfloat16)
            if pair == 0:
                send_up(sweep)
            if pair == height // 2 - 1:
                send_down(sweep)

    def run(items):
        for item in items:
            item()

    def turn(slot, products, early, late):
        count = len(products)
        shares = [[] for _ in products]
        for place, item in enumerate(early):
            shares[place * (count - 1) // len(early)].append(item)
        for place, item in enumerate(late):
            shares[count // 2 + place * (count // 2) // len(late)].append(item)
        for m, make in enumerate(products):
            prods[slot, m] = make()
            run(shares[m])

    def plan():
        top = height // 2 - 1
        middle = [("A", (index, index + 1)) for index in range(2, height, 2)]
        inner = [("B", pair) for pair in range(1, top)]
        ends = [("A", (0, 1)), ("A", (height, height + 1)), ("B", 0), ("B", top)]
        swapped = [ends[1], ends[0], ends[3], ends[2]]
        again = middle[1:2] + middle[:1] + middle[2:]
        return [(0, *part) for part in middle + inner + ends] + [
            (sweep, *part) for sweep in range(1, ITERS) for part in again + inner + swapped
        ]

    def all_turns():
        turns = plan()
        built = set()

        def missing(place):
            if place >= len(turns) or turns[place][1] != "A":
                return []
            sweep, _, pair = turns[place]
            rows = [index for index in range(pair[0], pair[1] + 3)]
            found = []
            for index in rows:
                both = (index - index % 2, index - index % 2 + 1)
                if (sweep, both) not in built:
                    built.add((sweep, both))
                    found.append((sweep, both))
            return found

        for sweep, pair in missing(0):
            run(build_items(sweep, pair))
        run(weight_items(raw_one, u_one, 4))
        after = []
        waiting = []
        for place, (sweep, kind, pair) in enumerate(turns):
            slot = place % 2
            for missed in missing(place):
                run(build_items(*missed))
            late = []
            for coming in missing(place + 1):
                late += build_items(*coming)
            if place == 0:
                waiting = weight_items(raw_two, u_two, 7)
                loads[7].start()
                loads[8].start()
                loads[9].start()
            elif place + 1 < len(turns) and turns[place + 1][1] == "B":
                late, waiting = late + waiting, []
            else:
                late, waiting = late + waiting[:1], waiting[1:]
            if kind == "A":
                products = [
                    functools.partial(product, u_one, main_one, rest_one, m, pair, sweep)
                    for m in range(4)
                ]
            else:
                rows = (2 * pair, 2 * pair + 1)
                products = [
                    functools.partial(product, u_two, main_two, rest_two, m, rows)
                    for m in range(4)
                ]
            turn(slot, products, after, late)
            if kind == "A":
                after = activate_items(sweep, pair, slot)
            else:
                after = finish_items(sweep, rows, slot)
        run(after)

    def parted(out_of):
        down = lax.broadcasted_iota(jnp.int32, (width, width), 0)
        across = lax.broadcasted_iota(jnp.int32, (width, width), 1)
        place, column = (down, across) if out_of else (across, down)
        source = jnp.where(place < side, 2 * place, 2 * (place - side) + 1)
        return jnp.where(source == column, 1.0, 0.0).astype(jnp.bfloat16)

    def reorder(value, matrix):
        return jnp.dot(
            jnp.concatenate(split_three(value), axis=1),
            jnp.concatenate([matrix] * 3, axis=0),
            preferred_element_type=jnp.float32,
        )

    into = parted(False)
    loads[0].wait()
    ordered = reorder(x_ref[...].reshape(chans * height, width), into)
    turned[...] = ordered.reshape(chans, height, width)
    for row in range(height):
        value = turned[:, row, :]
        rows_f32[row] = value
        state_rows[row] = value
        xb_rows[0, row + 2] = value.astype(jnp.bfloat16)
    greeted = (steps - 1) + jnp.where(has_up, 1, 0) + jnp.where(has_down, 1, 0)
    pl.semaphore_wait(barrier, greeted)
    send_up(0)
    send_down(0)
    for load in loads[1:4]:
        load.wait()
    wide = (-feats) % 128
    parts = [
        part.astype(jnp.float32)
        for part in split_three(jnp.pad(embed_ref[...], ((0, 0), (0, wide))))
    ]
    line = lax.broadcasted_iota(jnp.int32, (128 - chans, feats + wide), 0)
    under = jnp.zeros((128 - chans, feats + wide), jnp.float32)
    for place, part in enumerate(parts):
        under = jnp.where(line == place, part, under)
    over = jnp.pad(lift_ref[...].astype(jnp.float32), ((0, 0), (0, wide)))
    stacked = jnp.transpose(jnp.concatenate([over, under], axis=0))[:feats]
    lift_rows[...] = (0.5 * stacked).astype(jnp.bfloat16)
    for m in range(4):
        none = jnp.zeros((feats, EXTRA), jnp.bfloat16)
        u_one[m, :, depth : depth + EXTRA] = lift_rows[:, :EXTRA] if m in (0, 3) else none
        u_two[m, :, depth : depth + EXTRA] = none

    all_turns()

    for pair in range(height // 2):
        wait_drift(ITERS - 1, pair)
    for row in range(height):
        turned[:, row, :] = drift_own[row] + earlier(ITERS - 1, row)
    total = reorder(turned[...].reshape(chans * height, width), parted(True))
    out_ref[0] = x_ref[...] + total.reshape(chans, height, width)

    for sweep in range(ITERS):
        up, down = halo_copies(sweep)

        @pl.when(has_up)
        def _():
            up.wait_send()

        @pl.when(has_down)
        def _():
            down.wait_send()

        for shift in range(1, steps):
            for pair in range(height // 2):

                @pl.when(tm + shift < steps)
                def _():
                    drift_copy(sweep, shift, pair).wait_send()


def solution(mesh):
    steps, tiles = mesh.shape["tm"], mesh.shape["space"]

    def per_device(
        first_state,
        time_embed,
        drift_scale,
        state_decay,
        lift_weight,
        conv_one,
        conv_two,
        project_weight,
    ):
        chans, height, width = first_state.shape
        feats = lift_weight.shape[0]
        main = feats // TILE * TILE
        rest = feats - main
        depth = 3 * feats
        side = width // 2
        lines = pl.cdiv(depth + EXTRA, 128)
        wide = (lines + 1 - lines % 2) * 128
        peers = max(steps - 1, 1)
        vmem = pl.BlockSpec(memory_space=pltpu.VMEM)
        smem = pl.BlockSpec(memory_space=pltpu.SMEM)
        hbm = pl.BlockSpec(memory_space=pltpu.HBM)
        return pl.pallas_call(
            functools.partial(kernel, steps, tiles),
            out_shape=jax.ShapeDtypeStruct((1, chans, height, width), jnp.float32),
            in_specs=[hbm, hbm, smem, smem, hbm, hbm, hbm, hbm],
            out_specs=vmem,
            scratch_shapes=[
                pltpu.VMEM((chans, height, width), jnp.float32),
                pltpu.VMEM((1, feats), jnp.float32),
                pltpu.VMEM((chans, feats), jnp.bfloat16),
                pltpu.VMEM((chans, feats), jnp.bfloat16),
                pltpu.VMEM((3, 3, feats, feats), jnp.bfloat16),
                pltpu.VMEM((3, 3, feats, feats), jnp.bfloat16),
                pltpu.VMEM((4, feats, wide), jnp.bfloat16),
                pltpu.VMEM((4, feats, wide), jnp.bfloat16),
                pltpu.VMEM((feats, 128), jnp.bfloat16),
                pltpu.VMEM((4, (height + 4) * main, side), jnp.bfloat16),
                pltpu.VMEM((4, (height + 4) * rest, side), jnp.bfloat16),
                pltpu.VMEM((4, (height + 2) * main, side), jnp.bfloat16),
                pltpu.VMEM((4, (height + 2) * rest, side), jnp.bfloat16),
                pltpu.VMEM((height + 2, feats, width), jnp.float32),
                pltpu.VMEM((2, 4, feats, width), jnp.float32),
                pltpu.VMEM((2, feats, 2 * width), jnp.bfloat16),
                pltpu.VMEM((chans, height, width), jnp.float32),
                pltpu.VMEM((height, chans, width), jnp.float32),
                pltpu.VMEM((height, chans, width), jnp.float32),
                pltpu.VMEM((ITERS, height + 4, chans, width), jnp.bfloat16),
                pltpu.VMEM((height, chans, width), jnp.float32),
                pltpu.VMEM((ITERS, height, chans, width), jnp.bfloat16),
                pltpu.VMEM((ITERS, peers, height, chans, width), jnp.bfloat16),
                pltpu.SemaphoreType.DMA((10,)),
                pltpu.SemaphoreType.DMA((ITERS, 2)),
                pltpu.SemaphoreType.DMA((ITERS, 2)),
                pltpu.SemaphoreType.DMA((ITERS, peers, height // 2)),
                pltpu.SemaphoreType.DMA((ITERS, peers, height // 2)),
            ],
            compiler_params=pltpu.CompilerParams(
                collective_id=0, has_side_effects=True, vmem_limit_bytes=67043328
            ),
        )(
            first_state,
            time_embed,
            drift_scale,
            state_decay,
            lift_weight.T,
            project_weight,
            conv_one,
            conv_two,
        )

    in_specs = (P(None, "space", None), P("tm", None), P("tm"), P("tm"), P(), P(), P(), P())
    return jax.shard_map(
        per_device,
        mesh=mesh,
        in_specs=in_specs,
        out_specs=P("tm", None, "space", None),
        check_vma=False,
    )
```

```python
import functools

import jax
import jax.numpy as jnp
from jax import lax
from jax.experimental import pallas as pl
from jax.experimental.pallas import tpu as pltpu
from jax.sharding import PartitionSpec as P

ITERS = 2
TILE = 256
EXTRA = 64
MESH = pl.DeviceIdType.MESH


def gate(half):
    return half + half * jnp.tanh(half)


def split_three(value):
    high = value.astype(jnp.bfloat16)
    left = value - high.astype(jnp.float32)
    mid = left.astype(jnp.bfloat16)
    low = (left - mid.astype(jnp.float32)).astype(jnp.bfloat16)
    return high, mid, low


def kernel(
    steps,
    tiles,
    x_hbm,
    embed_hbm,
    scale_hbm,
    decay_hbm,
    lift_hbm,
    project_hbm,
    conv_one_hbm,
    conv_two_hbm,
    out_ref,
    x_ref,
    embed_ref,
    lift_ref,
    project_ref,
    scale_ref,
    decay_ref,
    raw_one,
    raw_two,
    u_one,
    u_two,
    lift_rows,
    main_one,
    rest_one,
    main_two,
    rest_two,
    first,
    prods,
    act_three,
    turned,
    rows_f32,
    state_rows,
    xb_rows,
    drift_own,
    drift_out,
    drift_in,
    load_sem,
    halo_send,
    halo_recv,
    drift_send,
    drift_recv,
):
    chans, height, width = x_ref.shape
    feats = lift_ref.shape[1]
    side = width // 2
    main = feats // TILE * TILE
    rest = feats - main
    depth = 3 * feats
    chunk = 64
    tm = lax.axis_index("tm")
    space = lax.axis_index("space")
    has_up = space > 0
    has_down = space < tiles - 1

    pairs = [(x_hbm, x_ref), (embed_hbm, embed_ref), (lift_hbm, lift_ref)]
    pairs += [(project_hbm, project_ref), (scale_hbm, scale_ref), (decay_hbm, decay_ref)]
    pairs += [(conv_one_hbm.at[p], raw_one.at[p]) for p in range(3)]
    pairs += [(conv_two_hbm.at[p], raw_two.at[p]) for p in range(3)]
    loads = [pltpu.make_async_copy(a, b, load_sem.at[i]) for i, (a, b) in enumerate(pairs)]
    for load in loads[:9]:
        load.start()

    barrier = pltpu.get_barrier_semaphore()
    for shift in range(1, steps):
        other = lax.rem(tm + shift, steps)
        pl.semaphore_signal(barrier, inc=1, device_id=(other, space), device_id_type=MESH)

    @pl.when(has_up)
    def _():
        pl.semaphore_signal(barrier, inc=1, device_id=(tm, space - 1), device_id_type=MESH)

    @pl.when(has_down)
    def _():
        pl.semaphore_signal(barrier, inc=1, device_id=(tm, space + 1), device_id_type=MESH)

    def clear_halo(start):
        for sweep in range(ITERS):
            for index in (start, start + 1):
                xb_rows[sweep, index] = jnp.zeros((chans, width), jnp.bfloat16)

    @pl.when(space == 0)
    def _():
        clear_halo(0)

    @pl.when(space == tiles - 1)
    def _():
        clear_halo(height + 2)

    def halo_copies(sweep):
        up = pltpu.make_async_remote_copy(
            src_ref=xb_rows.at[sweep, pl.ds(2, 2)],
            dst_ref=xb_rows.at[sweep, pl.ds(height + 2, 2)],
            send_sem=halo_send.at[sweep, 0],
            recv_sem=halo_recv.at[sweep, 1],
            device_id=(tm, space - 1),
            device_id_type=MESH,
        )
        down = pltpu.make_async_remote_copy(
            src_ref=xb_rows.at[sweep, pl.ds(height, 2)],
            dst_ref=xb_rows.at[sweep, pl.ds(0, 2)],
            send_sem=halo_send.at[sweep, 1],
            recv_sem=halo_recv.at[sweep, 0],
            device_id=(tm, space + 1),
            device_id_type=MESH,
        )
        return up, down

    def send_up(sweep):
        @pl.when(has_up)
        def _():
            halo_copies(sweep)[0].start()

    def send_down(sweep):
        @pl.when(has_down)
        def _():
            halo_copies(sweep)[1].start()

    def drift_copy(sweep, shift, pair):
        return pltpu.make_async_remote_copy(
            src_ref=drift_out.at[sweep, pl.ds(2 * pair, 2)],
            dst_ref=drift_in.at[sweep, shift - 1, pl.ds(2 * pair, 2)],
            send_sem=drift_send.at[sweep, shift - 1, pair],
            recv_sem=drift_recv.at[sweep, shift - 1, pair],
            device_id=(tm + shift, space),
            device_id_type=MESH,
        )

    def send_drift(sweep, pair):
        for shift in range(1, steps):

            @pl.when(tm + shift < steps)
            def _():
                drift_copy(sweep, shift, pair).start()

    def wait_drift(sweep, pair):
        for shift in range(1, steps):

            @pl.when(tm >= shift)
            def _():
                drift_copy(sweep, shift, pair).wait_recv()

    def earlier(sweep, row):
        total = jnp.zeros((chans, width), jnp.float32)
        for shift in range(1, steps):
            part = drift_in[sweep, shift - 1, row].astype(jnp.float32)
            total = total + jnp.where(tm >= shift, part, 0.0)
        return total

    lane = lax.broadcasted_iota(jnp.int32, (chunk, side), 1)
    zero = jnp.zeros((), jnp.bfloat16)
    ones = jnp.ones((EXTRA - chans, side), jnp.bfloat16)

    def spread(mains, rests, index, start, even, odd):
        even, odd = even.astype(jnp.bfloat16), odd.astype(jnp.bfloat16)
        before = jnp.where(lane == 0, zero, pltpu.roll(odd, 1, 1))
        after = jnp.where(lane == side - 1, zero, pltpu.roll(even, side - 1, 1))
        parts = (before - odd, even + odd, odd - even, after - even)
        for m, part in enumerate(parts):
            if start < main:
                place = index * main + start
                mains[m, place : place + chunk, :] = part
            else:
                place = index * rest + start - main
                rests[m, place : place + chunk, :] = part

    def extra(sweep, index, odd):
        xb = xb_rows[sweep, index]
        return jnp.concatenate([xb[:, side:] if odd else xb[:, :side], ones], axis=0)

    def product(weight, mains, rests, m, pair, sweep=None):
        taken = []
        used = depth + EXTRA
        for index in pair:
            pieces = [
                mains[m, index * main : (index + 3) * main, :],
                rests[m, index * rest : (index + 3) * rest, :],
            ]
            if sweep is not None and m in (0, 3):
                pieces.append(extra(sweep, index + 1, m == 3))
            else:
                pieces.append(jnp.zeros((EXTRA, side), jnp.bfloat16))
            taken.append(jnp.concatenate(pieces, axis=0))
        return jnp.dot(
            weight[m, :, :used],
            jnp.concatenate(taken, axis=1),
            preferred_element_type=jnp.float32,
        )

    def lift(sweep, pair):
        tall = jnp.ones((128 - chans, 2 * width), jnp.bfloat16)
        xb = jnp.concatenate([xb_rows[sweep, index] for index in pair], axis=1)
        return jnp.dot(
            lift_rows[...],
            jnp.concatenate([xb, tall], axis=0),
            preferred_element_type=jnp.float32,
        )

    def build_items(sweep, pair):
        held = []

        def first_item():
            for index in pair:
                reach(sweep, index)
            held.append(lift(sweep, pair))

        def item(half, index, start):
            acts = []
            for lanes in (half * width, half * width + side):
                act = gate(held[0][start : start + chunk, lanes : lanes + side])
                if index < 2:
                    act = jnp.where(has_up, act, 0.0)
                if index >= height + 2:
                    act = jnp.where(has_down, act, 0.0)
                acts.append(act)
            spread(main_one, rest_one, index, start, *acts)

        return [first_item] + [
            functools.partial(item, half, index, start)
            for half, index in enumerate(pair)
            for start in range(0, feats, chunk)
        ]

    def joined(slot, half, start):
        lanes = slice(half * side, (half + 1) * side)
        m0, m1, m2, m3 = [prods[slot, m, start : start + chunk, lanes] for m in range(4)]
        return m0 + m1 + m2, m1 - m2 + m3

    def activate_items(sweep, pair, slot):
        def item(half, index, start):
            values = joined(slot, half, start)
            acts = []
            for place, value in enumerate(values):
                if 0 < index <= height:
                    first[index, start : start + chunk, place * side : (place + 1) * side] = value
                act = gate(value)
                if index == 0:
                    act = jnp.where(has_up, act, 0.0)
                if index == height + 1:
                    act = jnp.where(has_down, act, 0.0)
                acts.append(act)
            spread(main_two, rest_two, index, start, *acts)

        return [
            functools.partial(item, half, index, start)
            for half, index in enumerate(pair)
            for start in range(0, feats, chunk)
        ]

    def finish_items(sweep, pair, slot):
        def item(half, row, start):
            for place, value in enumerate(joined(slot, half, start)):
                lanes = slice(place * side, (place + 1) * side)
                act = gate(first[row + 1, start : start + chunk, lanes] + value)
                lanes = slice(half * width + place * side, half * width + (place + 1) * side)
                act_three[slot, start : start + chunk, lanes] = act.astype(jnp.bfloat16)

        def last():
            out = jnp.dot(
                project_ref[...], act_three[slot], preferred_element_type=jnp.float32
            )
            for half, row in enumerate(pair):
                part = out[:, half * width : (half + 1) * width]
                drift = scale_ref[0] * part - decay_ref[0] * state_rows[row]
                drift_out[sweep, row] = drift.astype(jnp.bfloat16)
                if sweep == ITERS - 1:
                    drift_own[row] = drift
            send_drift(sweep, pair[0] // 2)

        return [
            functools.partial(item, half, row, start)
            for half, row in enumerate(pair)
            for start in range(0, feats, chunk)
        ] + [last]

    def weight_items(raw, weight, number):
        def item(p, start):
            if start == 0:
                loads[number + p].wait()
            lines = slice(start, start + chunk)
            taps = [raw[p, q, lines] for q in range(3)]
            centre = taps[1].astype(jnp.float32)
            outer = taps[0].astype(jnp.float32) + taps[2].astype(jnp.float32)
            filtered = (
                half_of * taps[0],
                quarter * (outer + centre).astype(jnp.bfloat16),
                quarter * (outer - centre).astype(jnp.bfloat16),
                half_of * taps[2],
            )
            for m, value in enumerate(filtered):
                weight[m, lines, p * main : (p + 1) * main] = value[:, :main]
                place = 3 * main + p * rest
                weight[m, lines, place : place + rest] = value[:, main:]

        half_of = jnp.asarray(0.5, jnp.bfloat16)
        quarter = jnp.asarray(0.25, jnp.bfloat16)
        return [
            functools.partial(item, p, start)
            for p in range(3)
            for start in range(0, feats, chunk)
        ]

    reached = set()

    def reach(sweep, index):
        if index < 2:
            key = (sweep, "up")
        elif index >= height + 2:
            key = (sweep, "down")
        else:
            key = (sweep, index // 2 - 1)
        if key in reached:
            return
        reached.add(key)
        if index < 2:

            @pl.when(has_up)
            def _():
                halo_copies(sweep)[1].wait_recv()

        elif index >= height + 2:

            @pl.when(has_down)
            def _():
                halo_copies(sweep)[0].wait_recv()

        elif sweep > 0:
            pair = key[1]
            wait_drift(sweep - 1, pair)
            for row in (2 * pair, 2 * pair + 1):
                state = rows_f32[row] + earlier(sweep - 1, row)
                state_rows[row] = state
                xb_rows[sweep, row + 2] = state.astype(jnp.bfloat16)
            if pair == 0:
                send_up(sweep)
            if pair == height // 2 - 1:
                send_down(sweep)

    def run(items):
        for item in items:
            item()

    def turn(slot, products, early, late):
        count = len(products)
        shares = [[] for _ in products]
        for place, item in enumerate(early):
            shares[place * (count - 1) // len(early)].append(item)
        for place, item in enumerate(late):
            shares[count // 2 + place * (count // 2) // len(late)].append(item)
        for m, make in enumerate(products):
            prods[slot, m] = make()
            run(shares[m])

    def plan():
        top = height // 2 - 1
        middle = [("A", (index, index + 1)) for index in range(2, height, 2)]
        inner = [("B", pair) for pair in range(1, top)]
        ends = [("A", (0, 1)), ("A", (height, height + 1)), ("B", 0), ("B", top)]
        swapped = [ends[1], ends[0], ends[3], ends[2]]
        again = middle[1:2] + middle[:1] + middle[2:]
        return [(0, *part) for part in middle + inner + ends] + [
            (sweep, *part) for sweep in range(1, ITERS) for part in again + inner + swapped
        ]

    def all_turns():
        turns = plan()
        built = set()

        def missing(place):
            if place >= len(turns) or turns[place][1] != "A":
                return []
            sweep, _, pair = turns[place]
            rows = [index for index in range(pair[0], pair[1] + 3)]
            found = []
            for index in rows:
                both = (index - index % 2, index - index % 2 + 1)
                if (sweep, both) not in built:
                    built.add((sweep, both))
                    found.append((sweep, both))
            return found

        for sweep, pair in missing(0):
            run(build_items(sweep, pair))
        greeted = (steps - 1) + jnp.where(has_up, 1, 0) + jnp.where(has_down, 1, 0)
        pl.semaphore_wait(barrier, greeted)
        send_up(0)
        send_down(0)
        run(weight_items(raw_one, u_one, 6))
        after = []
        waiting = []
        for place, (sweep, kind, pair) in enumerate(turns):
            slot = place % 2
            for missed in missing(place):
                run(build_items(*missed))
            late = []
            for coming in missing(place + 1):
                late += build_items(*coming)
            if place == 0:
                waiting = weight_items(raw_two, u_two, 9)
                for load in loads[9:]:
                    load.start()
            elif place + 1 < len(turns) and turns[place + 1][1] == "B":
                late, waiting = late + waiting, []
            else:
                many = len(waiting) // 2
                late, waiting = late + waiting[:many], waiting[many:]
            if kind == "A":
                products = [
                    functools.partial(product, u_one, main_one, rest_one, m, pair, sweep)
                    for m in range(4)
                ]
            else:
                rows = (2 * pair, 2 * pair + 1)
                products = [
                    functools.partial(product, u_two, main_two, rest_two, m, rows)
                    for m in range(4)
                ]
            turn(slot, products, after, late)
            if kind == "A":
                after = activate_items(sweep, pair, slot)
            else:
                after = finish_items(sweep, rows, slot)
        run(after)

    def parted(out_of):
        down = lax.broadcasted_iota(jnp.int32, (width, width), 0)
        across = lax.broadcasted_iota(jnp.int32, (width, width), 1)
        place, column = (down, across) if out_of else (across, down)
        source = jnp.where(place < side, 2 * place, 2 * (place - side) + 1)
        return jnp.where(source == column, 1.0, 0.0).astype(jnp.bfloat16)

    def reorder(value, matrix):
        return jnp.dot(
            jnp.concatenate(split_three(value), axis=1),
            jnp.concatenate([matrix] * 3, axis=0),
            preferred_element_type=jnp.float32,
        )

    into = parted(False)
    loads[0].wait()
    ordered = reorder(x_ref[...].reshape(chans * height, width), into)
    turned[...] = ordered.reshape(chans, height, width)
    for row in range(height):
        value = turned[:, row, :]
        rows_f32[row] = value
        state_rows[row] = value
        xb_rows[0, row + 2] = value.astype(jnp.bfloat16)
    for load in loads[1:6]:
        load.wait()
    wide = (-feats) % 128
    parts = [
        part.astype(jnp.float32)
        for part in split_three(jnp.pad(embed_ref[...], ((0, 0), (0, wide))))
    ]
    line = lax.broadcasted_iota(jnp.int32, (128 - chans, feats + wide), 0)
    under = jnp.zeros((128 - chans, feats + wide), jnp.float32)
    for place, part in enumerate(parts):
        under = jnp.where(line == place, part, under)
    over = jnp.pad(lift_ref[...].astype(jnp.float32), ((0, 0), (0, wide)))
    stacked = jnp.transpose(jnp.concatenate([over, under], axis=0))[:feats]
    lift_rows[...] = (0.5 * stacked).astype(jnp.bfloat16)
    for m in range(4):
        none = jnp.zeros((feats, EXTRA), jnp.bfloat16)
        u_one[m, :, depth : depth + EXTRA] = lift_rows[:, :EXTRA] if m in (0, 3) else none
        u_two[m, :, depth : depth + EXTRA] = none

    all_turns()

    for pair in range(height // 2):
        wait_drift(ITERS - 1, pair)
    for row in range(height):
        turned[:, row, :] = drift_own[row] + earlier(ITERS - 1, row)
    total = reorder(turned[...].reshape(chans * height, width), parted(True))
    out_ref[0] = x_ref[...] + total.reshape(chans, height, width)

    for sweep in range(ITERS):
        up, down = halo_copies(sweep)

        @pl.when(has_up)
        def _():
            up.wait_send()

        @pl.when(has_down)
        def _():
            down.wait_send()

        for shift in range(1, steps):
            for pair in range(height // 2):

                @pl.when(tm + shift < steps)
                def _():
                    drift_copy(sweep, shift, pair).wait_send()


def solution(mesh):
    steps, tiles = mesh.shape["tm"], mesh.shape["space"]

    def per_device(
        first_state,
        time_embed,
        drift_scale,
        state_decay,
        lift_weight,
        conv_one,
        conv_two,
        project_weight,
    ):
        chans, height, width = first_state.shape
        feats = lift_weight.shape[0]
        main = feats // TILE * TILE
        rest = feats - main
        depth = 3 * feats
        side = width // 2
        lines = pl.cdiv(depth + EXTRA, 128)
        wide = (lines + 1 - lines % 2) * 128
        peers = max(steps - 1, 1)
        room = 4 * chans * height * width
        vmem = pl.BlockSpec(memory_space=pltpu.VMEM)
        hbm = pl.BlockSpec(memory_space=pltpu.HBM)
        return pl.pallas_call(
            functools.partial(kernel, steps, tiles),
            out_shape=pltpu.VMEM((1, chans, height, width), jnp.float32),
            in_specs=[hbm] * 8,
            out_specs=vmem,
            scratch_shapes=[
                pltpu.VMEM((chans, height, width), jnp.float32),
                pltpu.VMEM((1, feats), jnp.float32),
                pltpu.VMEM((chans, feats), jnp.bfloat16),
                pltpu.VMEM((chans, feats), jnp.bfloat16),
                pltpu.SMEM((1,), jnp.float32),
                pltpu.SMEM((1,), jnp.float32),
                pltpu.VMEM((3, 3, feats, feats), jnp.bfloat16),
                pltpu.VMEM((3, 3, feats, feats), jnp.bfloat16),
                pltpu.VMEM((4, feats, wide), jnp.bfloat16),
                pltpu.VMEM((4, feats, wide), jnp.bfloat16),
                pltpu.VMEM((feats, 128), jnp.bfloat16),
                pltpu.VMEM((4, (height + 4) * main, side), jnp.bfloat16),
                pltpu.VMEM((4, (height + 4) * rest, side), jnp.bfloat16),
                pltpu.VMEM((4, (height + 2) * main, side), jnp.bfloat16),
                pltpu.VMEM((4, (height + 2) * rest, side), jnp.bfloat16),
                pltpu.VMEM((height + 2, feats, width), jnp.float32),
                pltpu.VMEM((2, 4, feats, width), jnp.float32),
                pltpu.VMEM((2, feats, 2 * width), jnp.bfloat16),
                pltpu.VMEM((chans, height, width), jnp.float32),
                pltpu.VMEM((height, chans, width), jnp.float32),
                pltpu.VMEM((height, chans, width), jnp.float32),
                pltpu.VMEM((ITERS, height + 4, chans, width), jnp.bfloat16),
                pltpu.VMEM((height, chans, width), jnp.float32),
                pltpu.VMEM((ITERS, height, chans, width), jnp.bfloat16),
                pltpu.VMEM((ITERS, peers, height, chans, width), jnp.bfloat16),
                pltpu.SemaphoreType.DMA((12,)),
                pltpu.SemaphoreType.DMA((ITERS, 2)),
                pltpu.SemaphoreType.DMA((ITERS, 2)),
                pltpu.SemaphoreType.DMA((ITERS, peers, height // 2)),
                pltpu.SemaphoreType.DMA((ITERS, peers, height // 2)),
            ],
            compiler_params=pltpu.CompilerParams(
                collective_id=0, has_side_effects=True, vmem_limit_bytes=67043328 - room
            ),
        )(
            first_state,
            time_embed,
            drift_scale,
            state_decay,
            lift_weight.T,
            project_weight,
            conv_one,
            conv_two,
        )

    in_specs = (P(None, "space", None), P("tm", None), P("tm"), P("tm"), P(), P(), P(), P())
    return jax.shard_map(
        per_device,
        mesh=mesh,
        in_specs=in_specs,
        out_specs=P("tm", None, "space", None),
        check_vma=False,
    )
```

```python
import functools

import jax
import jax.numpy as jnp
from jax import lax
from jax.experimental import pallas as pl
from jax.experimental.pallas import tpu as pltpu
from jax.sharding import PartitionSpec as P

ITERS = 2
TILE = 256
EXTRA = 64
MESH = pl.DeviceIdType.MESH


def gate(half):
    return half + half * jnp.tanh(half)


def split_three(value):
    high = value.astype(jnp.bfloat16)
    left = value - high.astype(jnp.float32)
    mid = left.astype(jnp.bfloat16)
    low = (left - mid.astype(jnp.float32)).astype(jnp.bfloat16)
    return high, mid, low


def kernel(
    steps,
    tiles,
    x_hbm,
    embed_hbm,
    scale_hbm,
    decay_hbm,
    lift_hbm,
    project_hbm,
    conv_one_hbm,
    conv_two_hbm,
    out_ref,
    x_ref,
    embed_ref,
    lift_ref,
    project_ref,
    scale_ref,
    decay_ref,
    raw_one,
    raw_two,
    u_one,
    u_two,
    lift_rows,
    main_one,
    rest_one,
    main_two,
    rest_two,
    first,
    prods,
    act_three,
    turned,
    rows_f32,
    state_rows,
    xb_rows,
    drift_own,
    drift_out,
    drift_in,
    load_sem,
    halo_send,
    halo_recv,
    drift_send,
    drift_recv,
):
    chans, height, width = x_ref.shape
    feats = lift_ref.shape[1]
    side = width // 2
    main = feats // TILE * TILE
    rest = feats - main
    depth = 3 * feats
    chunk = 64
    tm = lax.axis_index("tm")
    space = lax.axis_index("space")
    has_up = space > 0
    has_down = space < tiles - 1

    pairs = [(x_hbm, x_ref), (embed_hbm, embed_ref), (lift_hbm, lift_ref)]
    pairs += [(project_hbm, project_ref), (scale_hbm, scale_ref), (decay_hbm, decay_ref)]
    pairs += [(conv_one_hbm.at[p], raw_one.at[p]) for p in range(3)]
    pairs += [(conv_two_hbm.at[p], raw_two.at[p]) for p in range(3)]
    loads = [pltpu.make_async_copy(a, b, load_sem.at[i]) for i, (a, b) in enumerate(pairs)]
    for load in loads[:9]:
        load.start()

    barrier = pltpu.get_barrier_semaphore()
    for shift in range(1, steps):
        other = lax.rem(tm + shift, steps)
        pl.semaphore_signal(barrier, inc=1, device_id=(other, space), device_id_type=MESH)

    @pl.when(has_up)
    def _():
        pl.semaphore_signal(barrier, inc=1, device_id=(tm, space - 1), device_id_type=MESH)

    @pl.when(has_down)
    def _():
        pl.semaphore_signal(barrier, inc=1, device_id=(tm, space + 1), device_id_type=MESH)

    def clear_halo(start):
        for sweep in range(ITERS):
            for index in (start, start + 1):
                xb_rows[sweep, index] = jnp.zeros((chans, width), jnp.bfloat16)

    @pl.when(space == 0)
    def _():
        clear_halo(0)

    @pl.when(space == tiles - 1)
    def _():
        clear_halo(height + 2)

    def halo_copies(sweep):
        up = pltpu.make_async_remote_copy(
            src_ref=xb_rows.at[sweep, pl.ds(2, 2)],
            dst_ref=xb_rows.at[sweep, pl.ds(height + 2, 2)],
            send_sem=halo_send.at[sweep, 0],
            recv_sem=halo_recv.at[sweep, 1],
            device_id=(tm, space - 1),
            device_id_type=MESH,
        )
        down = pltpu.make_async_remote_copy(
            src_ref=xb_rows.at[sweep, pl.ds(height, 2)],
            dst_ref=xb_rows.at[sweep, pl.ds(0, 2)],
            send_sem=halo_send.at[sweep, 1],
            recv_sem=halo_recv.at[sweep, 0],
            device_id=(tm, space + 1),
            device_id_type=MESH,
        )
        return up, down

    def send_up(sweep):
        @pl.when(has_up)
        def _():
            halo_copies(sweep)[0].start()

    def send_down(sweep):
        @pl.when(has_down)
        def _():
            halo_copies(sweep)[1].start()

    def drift_copy(sweep, shift, pair):
        return pltpu.make_async_remote_copy(
            src_ref=drift_out.at[sweep, pl.ds(2 * pair, 2)],
            dst_ref=drift_in.at[sweep, shift - 1, pl.ds(2 * pair, 2)],
            send_sem=drift_send.at[sweep, shift - 1, pair],
            recv_sem=drift_recv.at[sweep, shift - 1, pair],
            device_id=(tm + shift, space),
            device_id_type=MESH,
        )

    def send_drift(sweep, pair):
        for shift in range(1, steps):

            @pl.when(tm + shift < steps)
            def _():
                drift_copy(sweep, shift, pair).start()

    def wait_drift(sweep, pair):
        for shift in range(1, steps):

            @pl.when(tm >= shift)
            def _():
                drift_copy(sweep, shift, pair).wait_recv()

    def earlier(sweep, row):
        total = jnp.zeros((chans, width), jnp.float32)
        for shift in range(1, steps):
            part = drift_in[sweep, shift - 1, row].astype(jnp.float32)
            total = total + jnp.where(tm >= shift, part, 0.0)
        return total

    lane = lax.broadcasted_iota(jnp.int32, (chunk, side), 1)
    zero = jnp.zeros((), jnp.bfloat16)
    ones = jnp.ones((EXTRA - chans, side), jnp.bfloat16)

    def spread(mains, rests, index, start, even, odd):
        even, odd = even.astype(jnp.bfloat16), odd.astype(jnp.bfloat16)
        before = jnp.where(lane == 0, zero, pltpu.roll(odd, 1, 1))
        after = jnp.where(lane == side - 1, zero, pltpu.roll(even, side - 1, 1))
        parts = (before - odd, even + odd, odd - even, after - even)
        for m, part in enumerate(parts):
            if start < main:
                place = index * main + start
                mains[m, place : place + chunk, :] = part
            else:
                place = index * rest + start - main
                rests[m, place : place + chunk, :] = part

    def extra(sweep, index, odd):
        xb = xb_rows[sweep, index]
        return jnp.concatenate([xb[:, side:] if odd else xb[:, :side], ones], axis=0)

    def product(weight, mains, rests, m, pair, sweep=None, part=None):
        taken = []
        used = depth + EXTRA
        for index in pair:
            pieces = [
                mains[m, index * main : (index + 3) * main, :],
                rests[m, index * rest : (index + 3) * rest, :],
            ]
            if sweep is not None and m in (0, 3):
                pieces.append(extra(sweep, index + 1, m == 3))
            else:
                pieces.append(jnp.zeros((EXTRA, side), jnp.bfloat16))
            taken.append(jnp.concatenate(pieces, axis=0))
        return jnp.dot(
            weight[m, part, :used],
            jnp.concatenate(taken, axis=1),
            preferred_element_type=jnp.float32,
        )

    def lift(sweep, pair):
        tall = jnp.ones((128 - chans, 2 * width), jnp.bfloat16)
        xb = jnp.concatenate([xb_rows[sweep, index] for index in pair], axis=1)
        return jnp.dot(
            lift_rows[...],
            jnp.concatenate([xb, tall], axis=0),
            preferred_element_type=jnp.float32,
        )

    def build_items(sweep, pair):
        held = []

        def first_item():
            for index in pair:
                reach(sweep, index)
            held.append(lift(sweep, pair))

        def item(half, index, start):
            acts = []
            for lanes in (half * width, half * width + side):
                act = gate(held[0][start : start + chunk, lanes : lanes + side])
                if index < 2:
                    act = jnp.where(has_up, act, 0.0)
                if index >= height + 2:
                    act = jnp.where(has_down, act, 0.0)
                acts.append(act)
            spread(main_one, rest_one, index, start, *acts)

        return [first_item] + [
            functools.partial(item, half, index, start)
            for half, index in enumerate(pair)
            for start in range(0, feats, chunk)
        ]

    def joined(slot, half, start):
        lanes = slice(half * side, (half + 1) * side)
        m0, m1, m2, m3 = [prods[slot, m, start : start + chunk, lanes] for m in range(4)]
        return m0 + m1 + m2, m1 - m2 + m3

    def activate_items(sweep, pair, slot):
        def item(half, index, start):
            values = joined(slot, half, start)
            acts = []
            for place, value in enumerate(values):
                if 0 < index <= height:
                    first[index, start : start + chunk, place * side : (place + 1) * side] = value
                act = gate(value)
                if index == 0:
                    act = jnp.where(has_up, act, 0.0)
                if index == height + 1:
                    act = jnp.where(has_down, act, 0.0)
                acts.append(act)
            spread(main_two, rest_two, index, start, *acts)

        return [
            functools.partial(item, half, index, start)
            for half, index in enumerate(pair)
            for start in range(0, feats, chunk)
        ]

    def finish_items(sweep, pair, slot):
        def item(half, row, start):
            for place, value in enumerate(joined(slot, half, start)):
                lanes = slice(place * side, (place + 1) * side)
                act = gate(first[row + 1, start : start + chunk, lanes] + value)
                lanes = slice(half * width + place * side, half * width + (place + 1) * side)
                act_three[slot, start : start + chunk, lanes] = act.astype(jnp.bfloat16)

        def last():
            out = jnp.dot(
                project_ref[...], act_three[slot], preferred_element_type=jnp.float32
            )
            for half, row in enumerate(pair):
                part = out[:, half * width : (half + 1) * width]
                drift = scale_ref[0] * part - decay_ref[0] * state_rows[row]
                drift_out[sweep, row] = drift.astype(jnp.bfloat16)
                if sweep == ITERS - 1:
                    drift_own[row] = drift
            send_drift(sweep, pair[0] // 2)

        return [
            functools.partial(item, half, row, start)
            for half, row in enumerate(pair)
            for start in range(0, feats, chunk)
        ] + [last]

    def weight_items(raw, weight):
        def item(p, start):
            lines = slice(start, start + chunk)
            taps = [raw[p, q, lines] for q in range(3)]
            centre = taps[1].astype(jnp.float32)
            outer = taps[0].astype(jnp.float32) + taps[2].astype(jnp.float32)
            filtered = (
                half_of * taps[0],
                quarter * (outer + centre).astype(jnp.bfloat16),
                quarter * (outer - centre).astype(jnp.bfloat16),
                half_of * taps[2],
            )
            for m, value in enumerate(filtered):
                weight[m, lines, p * main : (p + 1) * main] = value[:, :main]
                place = 3 * main + p * rest
                weight[m, lines, place : place + rest] = value[:, main:]

        half_of = jnp.asarray(0.5, jnp.bfloat16)
        quarter = jnp.asarray(0.25, jnp.bfloat16)
        return [
            functools.partial(item, p, start)
            for p in range(3)
            for start in range(0, feats, chunk)
        ]

    reached = set()

    def reach(sweep, index):
        if index < 2:
            key = (sweep, "up")
        elif index >= height + 2:
            key = (sweep, "down")
        else:
            key = (sweep, index // 2 - 1)
        if key in reached:
            return
        reached.add(key)
        if index < 2:

            @pl.when(has_up)
            def _():
                halo_copies(sweep)[1].wait_recv()

        elif index >= height + 2:

            @pl.when(has_down)
            def _():
                halo_copies(sweep)[0].wait_recv()

        elif sweep > 0:
            pair = key[1]
            wait_drift(sweep - 1, pair)
            for row in (2 * pair, 2 * pair + 1):
                state = rows_f32[row] + earlier(sweep - 1, row)
                state_rows[row] = state
                xb_rows[sweep, row + 2] = state.astype(jnp.bfloat16)
            if pair == 0:
                send_up(sweep)
            if pair == height // 2 - 1:
                send_down(sweep)

    def run(items):
        for item in items:
            item()

    def mixed(some, others):
        whole = list(some)
        for place, item in enumerate(others):
            whole.insert((place + 1) * (len(some) + len(others)) // (len(others) + 1), item)
        return whole

    def turn(slot, products, early, late):
        count = len(products)
        shares = [[] for _ in products]
        for place, item in enumerate(early):
            shares[place * (count - 1) // len(early)].append(item)
        for place, item in enumerate(late):
            shares[count // 2 + place * (count // 2) // len(late)].append(item)
        size = feats // 2
        for m, make in enumerate(products):
            for place in range(2):
                lines = slice(place * size, (place + 1) * size)
                prods[slot, m, lines] = make(part=lines)
                some = len(shares[m]) // 2
                run(shares[m][some:] if place else shares[m][:some])

    def plan():
        top = height // 2 - 1
        middle = [("A", (index, index + 1)) for index in range(2, height, 2)]
        inner = [("B", pair) for pair in range(1, top)]
        ends = [("A", (0, 1)), ("A", (height, height + 1)), ("B", 0), ("B", top)]
        swapped = [ends[1], ends[0], ends[3], ends[2]]
        again = middle[1:2] + middle[:1] + middle[2:]
        return [(0, *part) for part in middle + inner + ends] + [
            (sweep, *part) for sweep in range(1, ITERS) for part in again + inner + swapped
        ]

    def all_turns():
        turns = plan()
        built = set()

        def missing(place):
            if place >= len(turns) or turns[place][1] != "A":
                return []
            sweep, _, pair = turns[place]
            rows = [index for index in range(pair[0], pair[1] + 3)]
            found = []
            for index in rows:
                both = (index - index % 2, index - index % 2 + 1)
                if (sweep, both) not in built:
                    built.add((sweep, both))
                    found.append((sweep, both))
            return found

        for sweep, pair in missing(0):
            run(build_items(sweep, pair))
        greeted = (steps - 1) + jnp.where(has_up, 1, 0) + jnp.where(has_down, 1, 0)
        pl.semaphore_wait(barrier, greeted)
        send_up(0)
        send_down(0)
        for load in loads[6:9]:
            load.wait()
        for load in loads[9:]:
            load.start()
        run(weight_items(raw_one, u_one))
        after = []
        waiting = []
        for place, (sweep, kind, pair) in enumerate(turns):
            slot = place % 2
            for missed in missing(place):
                run(build_items(*missed))
            late = []
            for coming in missing(place + 1):
                late += build_items(*coming)
            if place == 1:
                for load in loads[9:]:
                    load.wait()
                waiting = weight_items(raw_two, u_two)
                late = mixed(late, waiting[:5])
                after = mixed(after, waiting[5:7])
            if place == 2:
                late = mixed(late, waiting[7:12])
                after = mixed(after, waiting[12:])
            if kind == "A":
                products = [
                    functools.partial(product, u_one, main_one, rest_one, m, pair, sweep)
                    for m in range(4)
                ]
            else:
                rows = (2 * pair, 2 * pair + 1)
                products = [
                    functools.partial(product, u_two, main_two, rest_two, m, rows)
                    for m in range(4)
                ]
            turn(slot, products, after, late)
            if kind == "A":
                after = activate_items(sweep, pair, slot)
            else:
                after = finish_items(sweep, rows, slot)
        run(after)

    def parted(out_of):
        down = lax.broadcasted_iota(jnp.int32, (width, width), 0)
        across = lax.broadcasted_iota(jnp.int32, (width, width), 1)
        place, column = (down, across) if out_of else (across, down)
        source = jnp.where(place < side, 2 * place, 2 * (place - side) + 1)
        return jnp.where(source == column, 1.0, 0.0).astype(jnp.bfloat16)

    def reorder(value, matrix):
        return jnp.dot(
            jnp.concatenate(split_three(value), axis=1),
            jnp.concatenate([matrix] * 3, axis=0),
            preferred_element_type=jnp.float32,
        )

    into = parted(False)
    loads[0].wait()
    ordered = reorder(x_ref[...].reshape(chans * height, width), into)
    turned[...] = ordered.reshape(chans, height, width)
    for row in range(height):
        value = turned[:, row, :]
        rows_f32[row] = value
        state_rows[row] = value
        xb_rows[0, row + 2] = value.astype(jnp.bfloat16)
    for load in loads[1:6]:
        load.wait()
    wide = (-feats) % 128
    parts = [
        part.astype(jnp.float32)
        for part in split_three(jnp.pad(embed_ref[...], ((0, 0), (0, wide))))
    ]
    line = lax.broadcasted_iota(jnp.int32, (128 - chans, feats + wide), 0)
    under = jnp.zeros((128 - chans, feats + wide), jnp.float32)
    for place, part in enumerate(parts):
        under = jnp.where(line == place, part, under)
    over = jnp.pad(lift_ref[...].astype(jnp.float32), ((0, 0), (0, wide)))
    stacked = jnp.transpose(jnp.concatenate([over, under], axis=0))[:feats]
    lift_rows[...] = (0.5 * stacked).astype(jnp.bfloat16)
    for m in range(4):
        none = jnp.zeros((feats, EXTRA), jnp.bfloat16)
        u_one[m, :, depth : depth + EXTRA] = lift_rows[:, :EXTRA] if m in (0, 3) else none
        u_two[m, :, depth : depth + EXTRA] = none

    all_turns()

    for pair in range(height // 2):
        wait_drift(ITERS - 1, pair)
    for row in range(height):
        turned[:, row, :] = drift_own[row] + earlier(ITERS - 1, row)
    total = reorder(turned[...].reshape(chans * height, width), parted(True))
    out_ref[0] = x_ref[...] + total.reshape(chans, height, width)

    for sweep in range(ITERS):
        up, down = halo_copies(sweep)

        @pl.when(has_up)
        def _():
            up.wait_send()

        @pl.when(has_down)
        def _():
            down.wait_send()

        for shift in range(1, steps):
            for pair in range(height // 2):

                @pl.when(tm + shift < steps)
                def _():
                    drift_copy(sweep, shift, pair).wait_send()


def solution(mesh):
    steps, tiles = mesh.shape["tm"], mesh.shape["space"]

    def per_device(
        first_state,
        time_embed,
        drift_scale,
        state_decay,
        lift_weight,
        conv_one,
        conv_two,
        project_weight,
    ):
        chans, height, width = first_state.shape
        feats = lift_weight.shape[0]
        main = feats // TILE * TILE
        rest = feats - main
        depth = 3 * feats
        side = width // 2
        lines = pl.cdiv(depth + EXTRA, 128)
        wide = (lines + 1 - lines % 2) * 128
        peers = max(steps - 1, 1)
        room = 4 * chans * height * width
        vmem = pl.BlockSpec(memory_space=pltpu.VMEM)
        hbm = pl.BlockSpec(memory_space=pltpu.HBM)
        return pl.pallas_call(
            functools.partial(kernel, steps, tiles),
            out_shape=pltpu.VMEM((1, chans, height, width), jnp.float32),
            in_specs=[hbm] * 8,
            out_specs=vmem,
            scratch_shapes=[
                pltpu.VMEM((chans, height, width), jnp.float32),
                pltpu.VMEM((1, feats), jnp.float32),
                pltpu.VMEM((chans, feats), jnp.bfloat16),
                pltpu.VMEM((chans, feats), jnp.bfloat16),
                pltpu.SMEM((1,), jnp.float32),
                pltpu.SMEM((1,), jnp.float32),
                pltpu.VMEM((3, 3, feats, feats), jnp.bfloat16),
                pltpu.VMEM((3, 3, feats, feats), jnp.bfloat16),
                pltpu.VMEM((4, feats, wide), jnp.bfloat16),
                pltpu.VMEM((4, feats, wide), jnp.bfloat16),
                pltpu.VMEM((feats, 128), jnp.bfloat16),
                pltpu.VMEM((4, (height + 4) * main, side), jnp.bfloat16),
                pltpu.VMEM((4, (height + 4) * rest, side), jnp.bfloat16),
                pltpu.VMEM((4, (height + 2) * main, side), jnp.bfloat16),
                pltpu.VMEM((4, (height + 2) * rest, side), jnp.bfloat16),
                pltpu.VMEM((height + 2, feats, width), jnp.float32),
                pltpu.VMEM((2, 4, feats, width), jnp.float32),
                pltpu.VMEM((2, feats, 2 * width), jnp.bfloat16),
                pltpu.VMEM((chans, height, width), jnp.float32),
                pltpu.VMEM((height, chans, width), jnp.float32),
                pltpu.VMEM((height, chans, width), jnp.float32),
                pltpu.VMEM((ITERS, height + 4, chans, width), jnp.bfloat16),
                pltpu.VMEM((height, chans, width), jnp.float32),
                pltpu.VMEM((ITERS, height, chans, width), jnp.bfloat16),
                pltpu.VMEM((ITERS, peers, height, chans, width), jnp.bfloat16),
                pltpu.SemaphoreType.DMA((12,)),
                pltpu.SemaphoreType.DMA((ITERS, 2)),
                pltpu.SemaphoreType.DMA((ITERS, 2)),
                pltpu.SemaphoreType.DMA((ITERS, peers, height // 2)),
                pltpu.SemaphoreType.DMA((ITERS, peers, height // 2)),
            ],
            compiler_params=pltpu.CompilerParams(
                collective_id=0, has_side_effects=True, vmem_limit_bytes=67043328 - room
            ),
        )(
            first_state,
            time_embed,
            drift_scale,
            state_decay,
            lift_weight.T,
            project_weight,
            conv_one,
            conv_two,
        )

    in_specs = (P(None, "space", None), P("tm", None), P("tm"), P("tm"), P(), P(), P(), P())
    return jax.shard_map(
        per_device,
        mesh=mesh,
        in_specs=in_specs,
        out_specs=P("tm", None, "space", None),
        check_vma=False,
    )
```

```python
import functools

import jax
import jax.numpy as jnp
from jax import lax
from jax.experimental import pallas as pl
from jax.experimental.pallas import tpu as pltpu
from jax.sharding import PartitionSpec as P

ITERS = 2
TILE = 256
EXTRA = 64
MESH = pl.DeviceIdType.MESH


def gate(half):
    return half + half * jnp.tanh(half)


def split_three(value):
    high = value.astype(jnp.bfloat16)
    left = value - high.astype(jnp.float32)
    mid = left.astype(jnp.bfloat16)
    low = (left - mid.astype(jnp.float32)).astype(jnp.bfloat16)
    return high, mid, low


def kernel(
    steps,
    tiles,
    x_hbm,
    embed_hbm,
    scale_hbm,
    decay_hbm,
    lift_hbm,
    project_hbm,
    conv_one_hbm,
    conv_two_hbm,
    out_ref,
    x_ref,
    embed_ref,
    lift_ref,
    project_ref,
    scale_ref,
    decay_ref,
    raw_one,
    raw_two,
    u_one,
    u_two,
    lift_rows,
    main_one,
    rest_one,
    main_two,
    rest_two,
    first,
    prods,
    act_three,
    turned,
    rows_f32,
    state_rows,
    xb_rows,
    drift_own,
    drift_out,
    drift_in,
    load_sem,
    halo_send,
    halo_recv,
    drift_send,
    drift_recv,
):
    chans, height, width = x_ref.shape
    feats = lift_ref.shape[1]
    side = width // 2
    main = feats // TILE * TILE
    rest = feats - main
    depth = 3 * feats
    chunk = 64
    tm = lax.axis_index("tm")
    space = lax.axis_index("space")
    has_up = space > 0
    has_down = space < tiles - 1

    pairs = [(x_hbm, x_ref), (embed_hbm, embed_ref), (lift_hbm, lift_ref)]
    pairs += [(project_hbm, project_ref), (scale_hbm, scale_ref), (decay_hbm, decay_ref)]
    pairs += [(conv_one_hbm.at[p], raw_one.at[p]) for p in range(3)]
    pairs += [(conv_two_hbm.at[p], raw_two.at[p]) for p in range(3)]
    loads = [pltpu.make_async_copy(a, b, load_sem.at[i]) for i, (a, b) in enumerate(pairs)]
    for load in loads[:9]:
        load.start()

    barrier = pltpu.get_barrier_semaphore()
    for shift in range(1, steps):
        other = lax.rem(tm + shift, steps)
        pl.semaphore_signal(barrier, inc=1, device_id=(other, space), device_id_type=MESH)

    @pl.when(has_up)
    def _():
        pl.semaphore_signal(barrier, inc=1, device_id=(tm, space - 1), device_id_type=MESH)

    @pl.when(has_down)
    def _():
        pl.semaphore_signal(barrier, inc=1, device_id=(tm, space + 1), device_id_type=MESH)

    def clear_halo(start):
        for sweep in range(ITERS):
            for index in (start, start + 1):
                xb_rows[sweep, index] = jnp.zeros((chans, width), jnp.bfloat16)

    @pl.when(space == 0)
    def _():
        clear_halo(0)

    @pl.when(space == tiles - 1)
    def _():
        clear_halo(height + 2)

    def halo_copies(sweep):
        up = pltpu.make_async_remote_copy(
            src_ref=xb_rows.at[sweep, pl.ds(2, 2)],
            dst_ref=xb_rows.at[sweep, pl.ds(height + 2, 2)],
            send_sem=halo_send.at[sweep, 0],
            recv_sem=halo_recv.at[sweep, 1],
            device_id=(tm, space - 1),
            device_id_type=MESH,
        )
        down = pltpu.make_async_remote_copy(
            src_ref=xb_rows.at[sweep, pl.ds(height, 2)],
            dst_ref=xb_rows.at[sweep, pl.ds(0, 2)],
            send_sem=halo_send.at[sweep, 1],
            recv_sem=halo_recv.at[sweep, 0],
            device_id=(tm, space + 1),
            device_id_type=MESH,
        )
        return up, down

    def send_up(sweep):
        @pl.when(has_up)
        def _():
            halo_copies(sweep)[0].start()

    def send_down(sweep):
        @pl.when(has_down)
        def _():
            halo_copies(sweep)[1].start()

    def drift_copy(sweep, shift, pair):
        return pltpu.make_async_remote_copy(
            src_ref=drift_out.at[sweep, pl.ds(2 * pair, 2)],
            dst_ref=drift_in.at[sweep, shift - 1, pl.ds(2 * pair, 2)],
            send_sem=drift_send.at[sweep, shift - 1, pair],
            recv_sem=drift_recv.at[sweep, shift - 1, pair],
            device_id=(tm + shift, space),
            device_id_type=MESH,
        )

    def send_drift(sweep, pair):
        for shift in range(1, steps):

            @pl.when(tm + shift < steps)
            def _():
                drift_copy(sweep, shift, pair).start()

    def wait_drift(sweep, pair):
        for shift in range(1, steps):

            @pl.when(tm >= shift)
            def _():
                drift_copy(sweep, shift, pair).wait_recv()

    def earlier(sweep, row):
        total = jnp.zeros((chans, width), jnp.float32)
        for shift in range(1, steps):
            part = drift_in[sweep, shift - 1, row].astype(jnp.float32)
            total = total + jnp.where(tm >= shift, part, 0.0)
        return total

    lane = lax.broadcasted_iota(jnp.int32, (chunk, side), 1)
    zero = jnp.zeros((), jnp.bfloat16)
    ones = jnp.ones((EXTRA - chans, side), jnp.bfloat16)

    def spread(mains, rests, index, start, even, odd):
        even, odd = even.astype(jnp.bfloat16), odd.astype(jnp.bfloat16)
        before = jnp.where(lane == 0, zero, pltpu.roll(odd, 1, 1))
        after = jnp.where(lane == side - 1, zero, pltpu.roll(even, side - 1, 1))
        parts = (before - odd, even + odd, odd - even, after - even)
        for m, part in enumerate(parts):
            if start < main:
                place = index * main + start
                mains[m, place : place + chunk, :] = part
            else:
                place = index * rest + start - main
                rests[m, place : place + chunk, :] = part

    def extra(sweep, index, odd):
        xb = xb_rows[sweep, index]
        return jnp.concatenate([xb[:, side:] if odd else xb[:, :side], ones], axis=0)

    def product(weight, mains, rests, m, pair, sweep=None, part=None):
        taken = []
        used = depth + EXTRA
        for index in pair:
            pieces = [
                mains[m, index * main : (index + 3) * main, :],
                rests[m, index * rest : (index + 3) * rest, :],
            ]
            if sweep is not None and m in (0, 3):
                pieces.append(extra(sweep, index + 1, m == 3))
            else:
                pieces.append(jnp.zeros((EXTRA, side), jnp.bfloat16))
            taken.append(jnp.concatenate(pieces, axis=0))
        return jnp.dot(
            weight[m, part, :used],
            jnp.concatenate(taken, axis=1),
            preferred_element_type=jnp.float32,
        )

    def lift(sweep, pair):
        tall = jnp.ones((128 - chans, 2 * width), jnp.bfloat16)
        xb = jnp.concatenate([xb_rows[sweep, index] for index in pair], axis=1)
        return jnp.dot(
            lift_rows[...],
            jnp.concatenate([xb, tall], axis=0),
            preferred_element_type=jnp.float32,
        )

    def build_items(sweep, pair):
        held = []

        def first_item():
            for index in pair:
                reach(sweep, index)
            held.append(lift(sweep, pair))

        def item(half, index, start):
            acts = []
            for lanes in (half * width, half * width + side):
                act = gate(held[0][start : start + chunk, lanes : lanes + side])
                if index < 2:
                    act = jnp.where(has_up, act, 0.0)
                if index >= height + 2:
                    act = jnp.where(has_down, act, 0.0)
                acts.append(act)
            spread(main_one, rest_one, index, start, *acts)

        return [first_item] + [
            functools.partial(item, half, index, start)
            for half, index in enumerate(pair)
            for start in range(0, feats, chunk)
        ]

    def joined(slot, half, start):
        lanes = slice(half * side, (half + 1) * side)
        m0, m1, m2, m3 = [prods[slot, m, start : start + chunk, lanes] for m in range(4)]
        return m0 + m1 + m2, m1 - m2 + m3

    def activate_items(sweep, pair, slot):
        def item(half, index, start):
            values = joined(slot, half, start)
            acts = []
            for place, value in enumerate(values):
                if 0 < index <= height:
                    first[index, start : start + chunk, place * side : (place + 1) * side] = value
                act = gate(value)
                if index == 0:
                    act = jnp.where(has_up, act, 0.0)
                if index == height + 1:
                    act = jnp.where(has_down, act, 0.0)
                acts.append(act)
            spread(main_two, rest_two, index, start, *acts)

        return [
            functools.partial(item, half, index, start)
            for half, index in enumerate(pair)
            for start in range(0, feats, chunk)
        ]

    def finish_items(sweep, pair, slot):
        def item(half, row, start):
            for place, value in enumerate(joined(slot, half, start)):
                lanes = slice(place * side, (place + 1) * side)
                act = gate(first[row + 1, start : start + chunk, lanes] + value)
                lanes = slice(half * width + place * side, half * width + (place + 1) * side)
                act_three[slot, start : start + chunk, lanes] = act.astype(jnp.bfloat16)

        def last():
            out = jnp.dot(
                project_ref[...], act_three[slot], preferred_element_type=jnp.float32
            )
            for half, row in enumerate(pair):
                part = out[:, half * width : (half + 1) * width]
                drift = scale_ref[0] * part - decay_ref[0] * state_rows[row]
                drift_out[sweep, row] = drift.astype(jnp.bfloat16)
                if sweep == ITERS - 1:
                    drift_own[row] = drift
            send_drift(sweep, pair[0] // 2)

        return [
            functools.partial(item, half, row, start)
            for half, row in enumerate(pair)
            for start in range(0, feats, chunk)
        ] + [last]

    def weight_items(raw, weight):
        def item(p, start):
            lines = slice(start, start + chunk)
            taps = [raw[p, q, lines] for q in range(3)]
            centre = taps[1].astype(jnp.float32)
            outer = taps[0].astype(jnp.float32) + taps[2].astype(jnp.float32)
            filtered = (
                half_of * taps[0],
                quarter * (outer + centre).astype(jnp.bfloat16),
                quarter * (outer - centre).astype(jnp.bfloat16),
                half_of * taps[2],
            )
            for m, value in enumerate(filtered):
                weight[m, lines, p * main : (p + 1) * main] = value[:, :main]
                place = 3 * main + p * rest
                weight[m, lines, place : place + rest] = value[:, main:]

        half_of = jnp.asarray(0.5, jnp.bfloat16)
        quarter = jnp.asarray(0.25, jnp.bfloat16)
        return [
            functools.partial(item, p, start)
            for p in range(3)
            for start in range(0, feats, chunk)
        ]

    reached = set()

    def reach(sweep, index):
        if index < 2:
            key = (sweep, "up")
        elif index >= height + 2:
            key = (sweep, "down")
        else:
            key = (sweep, index // 2 - 1)
        if key in reached:
            return
        reached.add(key)
        if index < 2:

            @pl.when(has_up)
            def _():
                halo_copies(sweep)[1].wait_recv()

        elif index >= height + 2:

            @pl.when(has_down)
            def _():
                halo_copies(sweep)[0].wait_recv()

        elif sweep > 0:
            pair = key[1]
            wait_drift(sweep - 1, pair)
            for row in (2 * pair, 2 * pair + 1):
                state = rows_f32[row] + earlier(sweep - 1, row)
                state_rows[row] = state
                xb_rows[sweep, row + 2] = state.astype(jnp.bfloat16)
            if pair == 0:
                send_up(sweep)
            if pair == height // 2 - 1:
                send_down(sweep)

    def run(items):
        for item in items:
            item()

    def mixed(some, others):
        whole = list(some)
        for place, item in enumerate(others):
            whole.insert((place + 1) * (len(some) + len(others)) // (len(others) + 1), item)
        return whole

    def turn(slot, products, early, late):
        count = len(products)
        shares = [[] for _ in products]
        for place, item in enumerate(early):
            shares[place * (count - 1) // len(early)].append(item)
        for place, item in enumerate(late):
            shares[count // 2 + place * (count // 2) // len(late)].append(item)
        size = feats // 2
        for m, make in enumerate(products):
            for place in range(2):
                lines = slice(place * size, (place + 1) * size)
                prods[slot, m, lines] = make(part=lines)
                some = len(shares[m]) // 2
                run(shares[m][some:] if place else shares[m][:some])

    def plan():
        top = height // 2 - 1
        middle = [("A", (index, index + 1)) for index in range(2, height, 2)]
        inner = [("B", pair) for pair in range(1, top)]
        ends = [("A", (0, 1)), ("A", (height, height + 1)), ("B", 0), ("B", top)]
        swapped = [ends[1], ends[0], ends[3], ends[2]]
        again = middle[1:2] + middle[:1] + middle[2:]
        return [(0, *part) for part in middle + inner + ends] + [
            (sweep, *part) for sweep in range(1, ITERS) for part in again + inner + swapped
        ]

    def all_turns():
        turns = plan()
        built = set()

        def missing(place):
            if place >= len(turns) or turns[place][1] != "A":
                return []
            sweep, _, pair = turns[place]
            rows = [index for index in range(pair[0], pair[1] + 3)]
            found = []
            for index in rows:
                both = (index - index % 2, index - index % 2 + 1)
                if (sweep, both) not in built:
                    built.add((sweep, both))
                    found.append((sweep, both))
            return found

        for sweep, pair in missing(0):
            run(build_items(sweep, pair))
        greeted = (steps - 1) + jnp.where(has_up, 1, 0) + jnp.where(has_down, 1, 0)
        pl.semaphore_wait(barrier, greeted)
        send_up(0)
        send_down(0)
        for load in loads[6:9]:
            load.wait()
        for load in loads[9:]:
            load.start()
        run(weight_items(raw_one, u_one))
        after = []
        waiting = []
        for place, (sweep, kind, pair) in enumerate(turns):
            slot = place % 2
            for missed in missing(place):
                run(build_items(*missed))
            late = []
            for coming in missing(place + 1):
                late += build_items(*coming)
            if place == 1:
                for load in loads[9:]:
                    load.wait()
                waiting = weight_items(raw_two, u_two)
                late = mixed(late, waiting[:5])
                after = mixed(after, waiting[5:7])
            if place == 2:
                late = mixed(late, waiting[7:12])
                after = mixed(after, waiting[12:])
            if kind == "A":
                products = [
                    functools.partial(product, u_one, main_one, rest_one, m, pair, sweep)
                    for m in range(4)
                ]
            else:
                rows = (2 * pair, 2 * pair + 1)
                products = [
                    functools.partial(product, u_two, main_two, rest_two, m, rows)
                    for m in range(4)
                ]
            turn(slot, products, after, late)
            if kind == "A":
                after = activate_items(sweep, pair, slot)
            else:
                after = finish_items(sweep, rows, slot)
        run(after)

    def parted(out_of):
        down = lax.broadcasted_iota(jnp.int32, (width, width), 0)
        across = lax.broadcasted_iota(jnp.int32, (width, width), 1)
        place, column = (down, across) if out_of else (across, down)
        source = jnp.where(place < side, 2 * place, 2 * (place - side) + 1)
        return jnp.where(source == column, 1.0, 0.0).astype(jnp.bfloat16)

    def reorder(value, matrix):
        return jnp.dot(
            jnp.concatenate(split_three(value), axis=1),
            jnp.concatenate([matrix] * 3, axis=0),
            preferred_element_type=jnp.float32,
        )

    into = parted(False)
    loads[0].wait()
    ordered = reorder(x_ref[...].reshape(chans * height, width), into)
    turned[...] = ordered.reshape(chans, height, width)
    for row in range(height):
        value = turned[:, row, :]
        rows_f32[row] = value
        state_rows[row] = value
        xb_rows[0, row + 2] = value.astype(jnp.bfloat16)
    for load in loads[1:6]:
        load.wait()
    wide = (-feats) % 128
    parts = [
        part.astype(jnp.float32)
        for part in split_three(jnp.pad(embed_ref[...], ((0, 0), (0, wide))))
    ]
    line = lax.broadcasted_iota(jnp.int32, (128 - chans, feats + wide), 0)
    under = jnp.zeros((128 - chans, feats + wide), jnp.float32)
    for place, part in enumerate(parts):
        under = jnp.where(line == place, part, under)
    over = jnp.pad(lift_ref[...].astype(jnp.float32), ((0, 0), (0, wide)))
    stacked = jnp.transpose(jnp.concatenate([over, under], axis=0))[:feats]
    lift_rows[...] = (0.5 * stacked).astype(jnp.bfloat16)
    for m in range(4):
        none = jnp.zeros((feats, EXTRA), jnp.bfloat16)
        u_one[m, :, depth : depth + EXTRA] = lift_rows[:, :EXTRA] if m in (0, 3) else none
        u_two[m, :, depth : depth + EXTRA] = none

    all_turns()

    back = parted(True)
    for pair in list(range(1, height // 2)) + [0]:
        wait_drift(ITERS - 1, pair)
        rows = (2 * pair, 2 * pair + 1)
        totals = [drift_own[row] + earlier(ITERS - 1, row) for row in rows]
        total = reorder(jnp.concatenate(totals, axis=0), back)
        for place, row in enumerate(rows):
            part = total[place * chans : (place + 1) * chans]
            out_ref[0, :, row, :] = x_ref[:, row, :] + part

    for sweep in range(ITERS):
        up, down = halo_copies(sweep)

        @pl.when(has_up)
        def _():
            up.wait_send()

        @pl.when(has_down)
        def _():
            down.wait_send()

        for shift in range(1, steps):
            for pair in range(height // 2):

                @pl.when(tm + shift < steps)
                def _():
                    drift_copy(sweep, shift, pair).wait_send()


def solution(mesh):
    steps, tiles = mesh.shape["tm"], mesh.shape["space"]

    def per_device(
        first_state,
        time_embed,
        drift_scale,
        state_decay,
        lift_weight,
        conv_one,
        conv_two,
        project_weight,
    ):
        chans, height, width = first_state.shape
        feats = lift_weight.shape[0]
        main = feats // TILE * TILE
        rest = feats - main
        depth = 3 * feats
        side = width // 2
        lines = pl.cdiv(depth + EXTRA, 128)
        wide = (lines + 1 - lines % 2) * 128
        peers = max(steps - 1, 1)
        room = 4 * chans * height * width
        vmem = pl.BlockSpec(memory_space=pltpu.VMEM)
        hbm = pl.BlockSpec(memory_space=pltpu.HBM)
        return pl.pallas_call(
            functools.partial(kernel, steps, tiles),
            out_shape=pltpu.VMEM((1, chans, height, width), jnp.float32),
            in_specs=[hbm] * 8,
            out_specs=vmem,
            scratch_shapes=[
                pltpu.VMEM((chans, height, width), jnp.float32),
                pltpu.VMEM((1, feats), jnp.float32),
                pltpu.VMEM((chans, feats), jnp.bfloat16),
                pltpu.VMEM((chans, feats), jnp.bfloat16),
                pltpu.SMEM((1,), jnp.float32),
                pltpu.SMEM((1,), jnp.float32),
                pltpu.VMEM((3, 3, feats, feats), jnp.bfloat16),
                pltpu.VMEM((3, 3, feats, feats), jnp.bfloat16),
                pltpu.VMEM((4, feats, wide), jnp.bfloat16),
                pltpu.VMEM((4, feats, wide), jnp.bfloat16),
                pltpu.VMEM((feats, 128), jnp.bfloat16),
                pltpu.VMEM((4, (height + 4) * main, side), jnp.bfloat16),
                pltpu.VMEM((4, (height + 4) * rest, side), jnp.bfloat16),
                pltpu.VMEM((4, (height + 2) * main, side), jnp.bfloat16),
                pltpu.VMEM((4, (height + 2) * rest, side), jnp.bfloat16),
                pltpu.VMEM((height + 2, feats, width), jnp.float32),
                pltpu.VMEM((2, 4, feats, width), jnp.float32),
                pltpu.VMEM((2, feats, 2 * width), jnp.bfloat16),
                pltpu.VMEM((chans, height, width), jnp.float32),
                pltpu.VMEM((height, chans, width), jnp.float32),
                pltpu.VMEM((height, chans, width), jnp.float32),
                pltpu.VMEM((ITERS, height + 4, chans, width), jnp.bfloat16),
                pltpu.VMEM((height, chans, width), jnp.float32),
                pltpu.VMEM((ITERS, height, chans, width), jnp.bfloat16),
                pltpu.VMEM((ITERS, peers, height, chans, width), jnp.bfloat16),
                pltpu.SemaphoreType.DMA((12,)),
                pltpu.SemaphoreType.DMA((ITERS, 2)),
                pltpu.SemaphoreType.DMA((ITERS, 2)),
                pltpu.SemaphoreType.DMA((ITERS, peers, height // 2)),
                pltpu.SemaphoreType.DMA((ITERS, peers, height // 2)),
            ],
            compiler_params=pltpu.CompilerParams(
                collective_id=0, has_side_effects=True, vmem_limit_bytes=67043328 - room
            ),
        )(
            first_state,
            time_embed,
            drift_scale,
            state_decay,
            lift_weight.T,
            project_weight,
            conv_one,
            conv_two,
        )

    in_specs = (P(None, "space", None), P("tm", None), P("tm"), P("tm"), P(), P(), P(), P())
    return jax.shard_map(
        per_device,
        mesh=mesh,
        in_specs=in_specs,
        out_specs=P("tm", None, "space", None),
        check_vma=False,
    )
```
